256 devices in a mesh: dp: 8 (over x, z_hi), expert: 32 (over y, z_lo, core).
Axes of the slice: x: 4, y: 4, z: 8 (z_hi: 2, z_lo: 4; z = z_hi * 4 + z_lo), core: 2. Of those that a mesh axis runs over, the one named last changes fastest.
Arguments:
- tokens: bfloat16 [4096, 5120], P('expert', 'dp'), may hold values from -6 to 6
- route_ids: int32 [4096, 6], P('expert'), may hold values from 0 to 31, all different within a row; in each aligned block of 128 rows (0 to 127, 128 to 255, ...) at most 26 rows name the same one
- route_weights: float32 [4096, 6], P('expert'), may hold values from 0.2 to 1
- w_gate: bfloat16 [32, 5120, 1024], P('expert', 'dp'), may hold values from -0.078125 to 0.078125
- w_up: bfloat16 [32, 5120, 1024], P('expert', 'dp'), may hold values from -0.078125 to 0.078125
- w_down: bfloat16 [32, 1024, 5120], P('expert', None, 'dp'), may hold values from -0.1875 to 0.1875
- shared_gate: bfloat16 [5120, 1536], P(('dp', 'expert')), may hold values from -0.078125 to 0.078125
- shared_up: bfloat16 [5120, 1536], P(('dp', 'expert')), may hold values from -0.078125 to 0.078125
- shared_down: bfloat16 [1536, 5120], P('expert', 'dp'), may hold values from -0.15625 to 0.15625
- cotangent: bfloat16 [4096, 5120], P('expert', 'dp'), may hold values from -6 to 6
Outputs:
- output: bfloat16 [4096, 5120], P('expert', 'dp')
- d_tokens: bfloat16 [4096, 5120], P('expert', 'dp')
- grad_gate: bfloat16 [32, 5120, 1024], P('expert', 'dp')
- grad_up: bfloat16 [32, 5120, 1024], P('expert', 'dp')
- grad_down: bfloat16 [32, 1024, 5120], P('expert', None, 'dp')
- grad_shared_gate: bfloat16 [5120, 1536], P(('dp', 'expert'))
- grad_shared_up: bfloat16 [5120, 1536], P(('dp', 'expert'))
- grad_shared_down: bfloat16 [1536, 5120], P('expert', 'dp')
The draws below stay inside these ranges and needn't reach their ends.
Inputs may be any that keep to these rules, and one draw needn't show every extreme that they name: `route_ids`: each row names 6 different experts. Among the 128 rows of one device (the aligned blocks of 128 rows) no expert is named more than 26 times, and in some block one expert is named exactly 26 times.
All inputs are finite; a program needn't handle non-finite values.
Results may differ from the reference program's by a relative error of at most 0.006.
Values may be sent and summed in bfloat16 or wider, within the bound.
No kernel may reach another device: no remote copies, remote signals or barrier semaphores. Data moves between devices by JAX's collectives and lax.ppermute only.
A program may use at most 128 MiB of HBM per device.

```python
import math
import jax
import jax.numpy as jnp
import numpy as np
from jax import lax

D = 5120
FF_EXP = 1024
FF_SH = 1536
TOPK = 6
TOK_DEV = 128
EXPERTS = 32
CAP = 26
TOKENS = 4096
N_EXPERT = 32


def spiked(values, key, source, target, blocks, factor):
    def block_of(dim):
        return (jnp.arange(values.shape[dim]) // (values.shape[dim] // blocks)).reshape((-1,) + (1,) * (values.ndim - 1 - dim))

    one_side = jax.random.permutation(key, blocks)[block_of(target)]
    other_side = (block_of(target) + blocks // 2) % blocks
    return jnp.where((block_of(source) == one_side) | (block_of(source) == other_side), factor * values, values)


def levels(own_key, extent, pieces, least, high):
    loudness, own = 1.0, jax.random.fold_in(own_key, 6)
    for dim, shards_of in pieces:
        heights = jnp.exp(jax.random.uniform(jax.random.fold_in(own, dim), (shards_of,), jnp.float32, least / len(pieces), high / len(pieces)))
        loudness = loudness * jnp.repeat(heights, extent[dim] // shards_of).reshape([-1 if axis == dim else 1 for axis in range(len(extent))])
    return loudness


def routed_block(key, own, number, rows, amount, top, bound, lean):
    ranking = jax.random.permutation(key, amount)
    crowded, ordinary = load_shares(amount, rows * top, bound, lean, True), load_shares(amount, rows * top, bound, lean, False)
    places = jnp.arange(amount)

    def named(sizes, offset_by):
        used = int((sizes > 0).sum())
        fixed = max(1, used // 4)
        shifted = fixed + (places - fixed + offset_by * (used - fixed)) % max(1, amount - fixed)
        return jnp.zeros((amount,), jnp.int32).at[ranking[jnp.where(places < fixed, places, shifted)]].set(jnp.asarray(sizes, jnp.int32))

    sizes = jnp.where(number % 4 == 0, named(crowded, number // 4), named(ordinary, number - number // 4 - 1))
    mixed = jax.random.permutation(jax.random.fold_in(own, 3), amount)
    source_of, taker = mixed[0:amount // 2 * 2:2], mixed[1:amount // 2 * 2:2]
    slack = jnp.minimum(sizes[source_of] - 1, bound - sizes[taker]) // 2
    slack = jnp.where((source_of == ranking[0]) | (taker == ranking[0]) | (sizes[taker] == 0), 0, jnp.maximum(slack, 0))
    shifted = jax.random.randint(jax.random.fold_in(own, 4), (amount // 2,), 0, 1 << 20) % (slack + 1)
    sizes = sizes.at[source_of].add(-shifted).at[taker].add(shifted)
    labels = jnp.searchsorted(jnp.cumsum(sizes), jnp.arange(rows * top), side="right").astype(jnp.int32)
    grid = labels.reshape(top, rows).T
    grid = grid[jax.random.permutation(jax.random.fold_in(own, 1), rows)]
    offset_by = jax.random.randint(jax.random.fold_in(own, 2), (rows, 1), 0, top)
    return jnp.take_along_axis(grid, (jnp.arange(top)[None, :] + offset_by) % top, axis=1)


def load_shares(count, total, reach, slope, full):
    portions = [(1 << 20) // math.isqrt(standing ** slope) + 1 for standing in range(1, count + 1)]
    largest = reach if full else min(reach, max(-(-total // count), total * portions[0] // sum(portions)))
    least = 1 if total - largest >= count - 1 else 0
    given, spare = [largest] + [least] * (count - 1), total - largest - least * (count - 1)
    while spare > 0:
        movable = [i for i in range(1, count) if given[i] < largest] or [i for i in range(1, count) if given[i] < reach]
        pool, remaining = sum([portions[i] for i in movable]), spare
        for i in movable:
            extra = min(reach - given[i], max(1, remaining * portions[i] // pool), spare)
            given[i] = given[i] + extra
            spare = spare - extra
    return np.array(given)


def normal_values(key, extent, width, reach, split=(), held_as=jnp.bfloat16):
    values = width * jax.random.normal(key, extent, jnp.float32)
    if split:
        values = values * levels(key, extent, split, -0.22, 0.18)
    return jnp.clip(values, -reach, reach).astype(held_as)


def heavy_noise(key, extent, width, reach, shards, heavy, kind=jnp.bfloat16):
    values = width * jax.random.normal(key, extent, jnp.float32)
    if shards:
        values = values * levels(key, extent, shards, -0.22, 0.18)
    return jnp.clip(spiked(values, jax.random.fold_in(key, 3), *heavy), -reach, reach).astype(kind)


def setup_inputs(seed: int = 0) -> dict:
    key_of = jax.random.split(jax.random.key(seed), 11)
    tokens = heavy_noise(key_of[0], (TOKENS, D), 1.0, 6.0, ((0, 32), (1, 8)), (0, 1, 32, 2.75))
    route_ids_keys = jax.random.split(jax.random.fold_in(key_of[1], 1), TOKENS // TOK_DEV)
    route_ids_turns = jax.random.permutation(jax.random.fold_in(key_of[1], 3), TOKENS // TOK_DEV)
    route_ids = jax.vmap(lambda own, number: routed_block(jax.random.fold_in(key_of[1], 2), own, number, TOK_DEV, EXPERTS, TOPK, CAP, 1))(route_ids_keys, route_ids_turns).reshape((TOKENS, TOPK))
    route_weights = jnp.clip(0.2 + 0.8 * jax.random.uniform(key_of[2], (TOKENS, TOPK), jnp.float32) ** levels(key_of[2], (TOKENS, TOPK), ((0, 32),), -0.2, 0.2), 0.2, 1.0)
    w_gate = normal_values(key_of[3], (EXPERTS, D, FF_EXP), D ** -0.5, 0.078125, ((0, 32), (1, 8)))
    w_up = normal_values(key_of[4], (EXPERTS, D, FF_EXP), D ** -0.5, 0.078125, ((0, 32), (1, 8)))
    w_down = normal_values(key_of[5], (EXPERTS, FF_EXP, D), FF_EXP ** -0.5, 0.1875, ((0, 32), (2, 8)))
    shared_gate = normal_values(key_of[6], (D, FF_SH), D ** -0.5, 0.078125, ((0, 256),))
    shared_up = normal_values(key_of[7], (D, FF_SH), D ** -0.5, 0.078125, ((0, 256),))
    shared_down = normal_values(key_of[8], (FF_SH, D), FF_SH ** -0.5, 0.15625, ((0, 32), (1, 8)))
    cotangent = normal_values(key_of[9], (TOKENS, D), 1.0, 6.0, ((0, 32), (1, 8)))
    return dict(tokens=tokens, route_ids=route_ids, route_weights=route_weights, w_gate=w_gate, w_up=w_up, w_down=w_down, shared_gate=shared_gate, shared_up=shared_up, shared_down=shared_down, cotangent=cotangent)


def activate(preact, hidden_width):
    gate_pre = preact[:, :hidden_width]
    up_pre = preact[:, hidden_width:]
    return gate_pre * jax.nn.sigmoid(gate_pre) * up_pre

def activation_grad(preact, hidden_grad, hidden_width):
    gate_pre = preact[:, :hidden_width]
    up_pre = preact[:, hidden_width:]
    sigmoid_gate = jax.nn.sigmoid(gate_pre)
    grad_gate_pre = hidden_grad * up_pre * sigmoid_gate * (1.0 + gate_pre * (1.0 - sigmoid_gate))
    grad_up_pre = hidden_grad * (gate_pre * sigmoid_gate)
    return jnp.concatenate([grad_gate_pre, grad_up_pre], axis=1).astype(jnp.bfloat16)

def slot_tables(flat_ids, experts, capacity):
    slot_total = flat_ids.shape[0]
    onehot = (flat_ids[:, None] == jnp.arange(experts, dtype=jnp.int32)[None, :]).astype(jnp.int32)
    before = jnp.cumsum(onehot, axis=0) - onehot
    position = lax.optimization_barrier(jnp.sum(before * onehot, axis=1))
    target = flat_ids * capacity + position
    slot_table = jnp.zeros((experts * capacity,), jnp.int32).at[target].set(jnp.arange(slot_total, dtype=jnp.int32) + 1)
    return (target, slot_table)

def contract(left, right, left_dim, right_dim):
    return lax.dot_general(left, right, (((left_dim,), (right_dim,)), ((), ())), preferred_element_type=jnp.float32)

def reference(tokens, route_ids, route_weights, w_gate, w_up, w_down, shared_gate, shared_up, shared_down, cotangent):
    per_block = TOK_DEV * TOPK
    total_slots = N_EXPERT * per_block
    targets, tables = jax.vmap(lambda block_ids: slot_tables(block_ids, EXPERTS, CAP))(route_ids.reshape(N_EXPERT, per_block))
    block_base = (jnp.arange(N_EXPERT, dtype=jnp.int32) * per_block)[:, None]
    global_slot = jnp.where(tables > 0, tables - 1 + block_base, total_slots).astype(jnp.int32)
    weight_flat = route_weights.reshape(-1)

    def one_expert(totals, inputs):
        out_slots, grad_slots = totals
        gate_weight, up_weight, down_weight, expert = inputs
        chosen = lax.dynamic_slice_in_dim(global_slot, expert * CAP, CAP, 1).reshape(-1)
        filled = (chosen < total_slots)[:, None]
        clamped = jnp.minimum(chosen, total_slots - 1)
        token_index = (clamped // TOPK).astype(jnp.int32)
        rows_in = jnp.where(filled, tokens[token_index], jnp.zeros((), jnp.bfloat16))
        joined = jnp.concatenate([gate_weight, up_weight], axis=1)
        preact = jnp.dot(rows_in, joined, preferred_element_type=jnp.float32)
        hidden = activate(preact, FF_EXP).astype(jnp.bfloat16)
        expert_out = jnp.dot(hidden, down_weight, preferred_element_type=jnp.float32).astype(jnp.bfloat16)
        slot_grad = (weight_flat[clamped][:, None] * cotangent[token_index].astype(jnp.float32)).astype(jnp.bfloat16)
        slot_grad = jnp.where(filled, slot_grad, jnp.zeros((), jnp.bfloat16))
        hidden_grad = contract(slot_grad, down_weight, 1, 1)
        pre_grad = activation_grad(preact, hidden_grad, FF_EXP)
        input_grad = contract(pre_grad, joined, 1, 1).astype(jnp.bfloat16)
        grad_join = contract(rows_in, pre_grad, 0, 0)
        grad_dn = contract(hidden, slot_grad, 0, 0)
        out_slots = out_slots.at[chosen].set(expert_out, mode='drop')
        grad_slots = grad_slots.at[chosen].set(input_grad, mode='drop')
        results = (grad_join[:, :FF_EXP].astype(jnp.bfloat16), grad_join[:, FF_EXP:].astype(jnp.bfloat16), grad_dn.astype(jnp.bfloat16))
        return ((out_slots, grad_slots), results)
    start_slots = jnp.zeros((total_slots, D), jnp.bfloat16)
    (out_slots, grad_slots), stacked = lax.scan(one_expert, (start_slots, start_slots), (w_gate, w_up, w_down, jnp.arange(EXPERTS, dtype=jnp.int32)))
    grad_gate, grad_up, grad_down = stacked
    routed_out = lax.optimization_barrier(jnp.sum(out_slots.astype(jnp.float32).reshape(TOKENS, TOPK, D) * route_weights[:, :, None], axis=1))
    routed_grad = lax.optimization_barrier(jnp.sum(grad_slots.astype(jnp.float32).reshape(TOKENS, TOPK, D), axis=1))
    common_join = jnp.concatenate([shared_gate, shared_up], axis=1)
    common_pre = jnp.dot(tokens, common_join, preferred_element_type=jnp.float32)
    common_hidden = activate(common_pre, FF_SH).astype(jnp.bfloat16)
    common_out = jnp.dot(common_hidden, shared_down, preferred_element_type=jnp.float32)
    output = (common_out + routed_out).astype(jnp.bfloat16)
    common_grad = contract(cotangent, shared_down, 1, 1)
    common_pregrad = activation_grad(common_pre, common_grad, FF_SH)
    common_input = contract(common_pregrad, common_join, 1, 1)
    d_tokens = (common_input + routed_grad).astype(jnp.bfloat16)
    join_sum = contract(tokens, common_pregrad, 0, 0)
    down_sum = contract(common_hidden, cotangent, 0, 0)
    grad_shared_gate = join_sum[:, :FF_SH].astype(jnp.bfloat16)
    grad_shared_up = join_sum[:, FF_SH:].astype(jnp.bfloat16)
    grad_shared_down = down_sum.astype(jnp.bfloat16)
    return (output, d_tokens, grad_gate, grad_up, grad_down, grad_shared_gate, grad_shared_up, grad_shared_down)
```

```python
import jax
import jax.numpy as jnp
from jax import lax
from jax.sharding import Mesh, PartitionSpec as P

BF16 = jnp.bfloat16
F32 = jnp.float32
NX, NZH, NY, NZL, NC = 4, 2, 4, 4, 2
DP = ("x", "zh")
YC = ("y", "c")
NDP = NX * NZH
NYC = NY * NC


def shift(value, axis, by, size):
    return lax.ppermute(value, axis, [(i, (i + by) % size) for i in range(size)])


def dot(left, right, left_dim=1, right_dim=0):
    return lax.dot_general(
        left, right, (((left_dim,), (right_dim,)), ((), ())), preferred_element_type=F32
    )


def activate(gate, up):
    return gate * jax.nn.sigmoid(gate) * up


def activation_grad(gate, up, hidden_grad):
    s = jax.nn.sigmoid(gate)
    return (
        hidden_grad * up * s * (1.0 + gate * (1.0 - s)),
        hidden_grad * (gate * s),
    )


def chunk_index(k, r):
    return ((lax.axis_index("x") + k) % NX) * NZH + (lax.axis_index("zh") + r) % NZH


def reduce_over_dp(part):
    to_far = shift(part(2, 1).astype(BF16), "x", 1, NX)
    back_far = shift(part(3, 1).astype(BF16), "x", -1, NX)
    to_own = shift(part(2, 0).astype(BF16), "x", -1, NX)
    on_far = shift((part(1, 1) + to_far.astype(F32)).astype(BF16), "x", 1, NX)
    far = part(0, 1) + on_far.astype(F32) + back_far.astype(F32)
    across = shift(far.astype(BF16), "zh", 1, NZH)
    on_own = shift(part(1, 0).astype(BF16), "x", 1, NX)
    back_own = shift((part(3, 0) + to_own.astype(F32)).astype(BF16), "x", -1, NX)
    own = part(0, 0) + on_own.astype(F32) + back_own.astype(F32)
    return own + across.astype(F32)


def gather_over_dp(own):
    rows, width = own.shape
    cut = (rows // 2 + 7) // 8 * 8
    full = jnp.zeros((NDP, rows, width), BF16)

    def put(full, piece, k, r, row=0):
        return lax.dynamic_update_slice(full, piece[None], (chunk_index(k, r), row, 0))

    other = shift(own, "zh", 1, NZH)
    full = put(full, own, 0, 0)
    for r, mine in ((0, own), (1, other)):
        if r:
            full = put(full, mine, 0, 1)
        before = shift(mine, "x", 1, NX)
        after = shift(mine, "x", -1, NX)
        top = shift(before[:cut], "x", 1, NX)
        low = shift(after[cut:], "x", -1, NX)
        full = put(full, before, 3, r)
        full = put(full, after, 1, r)
        full = put(full, top, 2, r)
        full = put(full, low, 2, r, cut)
    return full


def rows_of(blocks, k, r):
    return lax.dynamic_index_in_dim(blocks, chunk_index(k, r), 0, keepdims=False)


def all_near(value):
    return [value] + [shift(value, "zl", k, NZL) for k in range(1, NZL)]


def sum_near(blocks):
    total = blocks[0]
    for k in range(1, NZL):
        total = total + shift(blocks[k].astype(BF16), "zl", -k, NZL).astype(F32)
    return total


def to_owner(rows):
    return lax.all_to_all(rows, YC, 0, 0, tiled=True)


def body(
    tokens,
    route_ids,
    route_weights,
    w_gate,
    w_up,
    w_down,
    shared_gate,
    shared_up,
    shared_down,
    cotangent,
):
    tok_rows, top_count = route_ids.shape
    features = tokens.shape[1]
    hidden_exp = w_gate.shape[2]
    hidden_sh = shared_gate.shape[1]
    experts = NYC * NZL
    average = tok_rows * top_count // experts
    capacity = average + max(average // 12, 2)
    span = NZL * capacity
    all_rows = NZL * tok_rows
    zl = lax.axis_index("zl")

    routes = jnp.concatenate([route_ids.T.astype(F32), route_weights.T], axis=0)
    routes_all = jnp.concatenate(all_near(routes), axis=1)
    cot_all = jnp.concatenate(all_near(cotangent), axis=0)
    tok_all = jnp.concatenate(all_near(tokens), axis=0)

    ids = routes_all[:top_count].astype(jnp.int32)
    weights = routes_all[top_count:]
    place = jnp.arange(NYC, dtype=jnp.int32)
    expert = (place // NC) * (NZL * NC) + zl * NC + place % NC
    hit = ids[None] == expert[:, None, None]
    member = jnp.sum(hit.astype(F32), axis=1)
    weight = jnp.sum(jnp.where(hit, weights[None], 0.0), axis=1)
    earlier = (
        lax.broadcasted_iota(jnp.int32, (tok_rows, tok_rows), 0)
        < lax.broadcasted_iota(jnp.int32, (tok_rows, tok_rows), 1)
    ).astype(BF16)
    before = dot(member.astype(BF16).reshape(NYC * NZL, tok_rows), earlier)
    before = before.reshape(NYC, all_rows).astype(jnp.int32)
    block = jnp.arange(all_rows, dtype=jnp.int32) // tok_rows
    slot = jnp.where(member > 0, before + block[None] * capacity, -1)
    chosen = slot[:, None, :] == lax.broadcasted_iota(jnp.int32, (NYC, span, all_rows), 1)
    weight_high = weight.astype(BF16)
    weight_low = (weight - weight_high.astype(F32)).astype(BF16)
    zero = jnp.zeros((), BF16)
    pick = chosen.astype(BF16).reshape(NYC * span, all_rows)
    pick_high = jnp.where(chosen, weight_high[:, None, :], zero).reshape(NYC * span, all_rows)
    pick_low = jnp.where(chosen, weight_low[:, None, :], zero).reshape(NYC * span, all_rows)

    grad_rows = (dot(pick_high, cot_all) + dot(pick_low, cot_all)).astype(BF16)
    grad_in = to_owner(grad_rows.reshape(NYC, span, features))
    send_rows = dot(pick, tok_all).astype(BF16)
    arrived = to_owner(send_rows.reshape(NYC, span, features))

    joined = jnp.concatenate([w_gate[0], w_up[0]], axis=1)
    down = w_down[0]

    part_sh = hidden_sh // NZL
    piece = part_sh // NY
    rows_sh = shared_gate.shape[0]

    def by_zl(w):
        w = w.reshape(rows_sh, NY, NZL, piece).transpose(2, 0, 1, 3)
        return w.reshape(NZL, rows_sh, part_sh)

    both = jnp.concatenate([by_zl(shared_gate), by_zl(shared_up)], axis=2)
    both = lax.all_to_all(both, "zl", 0, 0, tiled=True).reshape(NZL * rows_sh, 2 * part_sh)
    both = lax.all_gather(both, YC, axis=0, tiled=True)
    sh_down = lax.all_gather(shared_down, YC, axis=0, tiled=True)
    feature = jnp.arange(features, dtype=jnp.int32)
    f_row, f_c = feature % rows_sh, feature // rows_sh % NC
    f_zl, f_y = feature // (rows_sh * NC) % NZL, feature // (rows_sh * NC * NZL)
    came = ((f_y * NC + f_c) * NZL + f_zl) * rows_sh + f_row
    order = (
        came[:, None] == lax.broadcasted_iota(jnp.int32, (features, features), 1)
    ).astype(BF16)
    sh_join = dot(order, both).astype(BF16)

    tok_blocks = tok_all.reshape(NDP, all_rows // NDP, features)
    cot_blocks = cot_all.reshape(NDP, all_rows // NDP, features)

    def shared_part(k, r):
        return jnp.concatenate(
            [
                dot(rows_of(tok_blocks, k, r), sh_join),
                dot(rows_of(cot_blocks, k, r), sh_down, 1, 1),
            ],
            axis=1,
        )

    sh_own = reduce_over_dp(shared_part)
    sh_gate_pre = sh_own[:, :part_sh]
    sh_up_pre = sh_own[:, part_sh : 2 * part_sh]
    sh_hidden = activate(sh_gate_pre, sh_up_pre)
    sh_pregrad = activation_grad(sh_gate_pre, sh_up_pre, sh_own[:, 2 * part_sh :])
    sh_full = gather_over_dp(
        jnp.concatenate([sh_hidden, *sh_pregrad], axis=1).astype(BF16)
    ).reshape(all_rows, 3 * part_sh)
    sh_hidden_full = sh_full[:, :part_sh]
    sh_pregrad_full = sh_full[:, part_sh:]

    grad_own = reduce_over_dp(lambda k, r: dot(rows_of(grad_in, k, r), down, 1, 1))
    pre_own = reduce_over_dp(lambda k, r: dot(rows_of(arrived, k, r), joined))
    gate_pre, up_pre = pre_own[:, :hidden_exp], pre_own[:, hidden_exp:]
    hidden_own = activate(gate_pre, up_pre).astype(BF16)
    pregrad_own = jnp.concatenate(
        activation_grad(gate_pre, up_pre, grad_own), axis=1
    ).astype(BF16)
    slots = NYC * span
    hidden_full = gather_over_dp(hidden_own).reshape(slots, hidden_exp)
    pregrad_full = gather_over_dp(pregrad_own).reshape(slots, 2 * hidden_exp)

    expert_out = dot(hidden_full, down).astype(BF16)
    returned = to_owner(expert_out.reshape(NYC, span, features)).reshape(slots, features)
    out_part = (
        dot(sh_hidden_full, sh_down)
        + dot(pick_high, returned, 0, 0)
        + dot(pick_low, returned, 0, 0)
    )
    output = sum_near(list(out_part.reshape(NZL, tok_rows, features))).astype(BF16)

    input_grad = dot(pregrad_full, joined, 1, 1).astype(BF16)
    grad_back = to_owner(input_grad.reshape(NYC, span, features)).reshape(slots, features)
    tok_part = dot(sh_pregrad_full, sh_join, 1, 1) + dot(pick, grad_back, 0, 0)
    d_tokens = sum_near(list(tok_part.reshape(NZL, tok_rows, features))).astype(BF16)

    grad_down = dot(hidden_full, grad_in.reshape(slots, features), 0, 0).astype(BF16)[None]
    grad_join = dot(arrived.reshape(slots, features), pregrad_full, 0, 0).astype(BF16)
    grad_gate = grad_join[None, :, :hidden_exp]
    grad_up = grad_join[None, :, hidden_exp:]

    sh_grad = dot(tok_all, sh_pregrad_full, 0, 0).astype(BF16)
    sh_grad = dot(order, sh_grad, 0, 0).astype(BF16)
    sh_grad = to_owner(sh_grad.reshape(NYC, NZL * rows_sh, 2 * part_sh))
    sh_grad = jnp.sum(sh_grad.astype(F32), axis=0).astype(BF16)
    sh_grad = lax.all_to_all(
        sh_grad.reshape(NZL, rows_sh, 2 * part_sh), "zl", 0, 0, tiled=True
    )

    def from_zl(g):
        g = g.reshape(NZL, rows_sh, NY, piece).transpose(1, 2, 0, 3)
        return g.reshape(rows_sh, hidden_sh)

    grad_shared_gate = from_zl(sh_grad[:, :, :part_sh])
    grad_shared_up = from_zl(sh_grad[:, :, part_sh:])
    sh_down_grad = dot(sh_hidden_full, cot_all, 0, 0).astype(BF16)
    sh_down_grad = to_owner(sh_down_grad.reshape(NYC, part_sh // NYC, features))
    grad_shared_down = jnp.sum(sh_down_grad.astype(F32), axis=0).astype(BF16)
    return (
        output,
        d_tokens,
        grad_gate,
        grad_up,
        grad_down,
        grad_shared_gate,
        grad_shared_up,
        grad_shared_down,
    )


def solution(mesh):
    parts = Mesh(
        mesh.devices.reshape(NX, NZH, NY, NZL, NC), ("x", "zh", "y", "zl", "c")
    )
    dp, expert = ("x", "zh"), ("y", "zl", "c")
    in_specs = (
        P(expert, dp),
        P(expert, None),
        P(expert, None),
        P(expert, dp, None),
        P(expert, dp, None),
        P(expert, None, dp),
        P(dp + expert, None),
        P(dp + expert, None),
        P(expert, dp),
        P(expert, dp),
    )
    out_specs = (
        P(expert, dp),
        P(expert, dp),
        P(expert, dp, None),
        P(expert, dp, None),
        P(expert, None, dp),
        P(dp + expert, None),
        P(dp + expert, None),
        P(expert, dp),
    )
    return jax.shard_map(
        body, mesh=parts, in_specs=in_specs, out_specs=out_specs, check_vma=False
    )
```

```python
import jax
import jax.numpy as jnp
from jax import lax
from jax.sharding import Mesh, PartitionSpec as P

BF16 = jnp.bfloat16
F32 = jnp.float32
NX, NZH, NY, NZL, NC = 4, 2, 4, 4, 2
DP = ("x", "zh")
YC = ("y", "c")
NDP = NX * NZH
NYC = NY * NC


def shift(value, axis, by, size):
    return lax.ppermute(value, axis, [(i, (i + by) % size) for i in range(size)])


def dot(left, right, left_dim=1, right_dim=0):
    return lax.dot_general(
        left, right, (((left_dim,), (right_dim,)), ((), ())), preferred_element_type=F32
    )


def activate(gate, up):
    return gate * jax.nn.sigmoid(gate) * up


def activation_grad(gate, up, hidden_grad):
    s = jax.nn.sigmoid(gate)
    return (
        hidden_grad * up * s * (1.0 + gate * (1.0 - s)),
        hidden_grad * (gate * s),
    )


def chunk_index(k, r):
    return ((lax.axis_index("x") + k) % NX) * NZH + (lax.axis_index("zh") + r) % NZH


def reduce_over_dp(*addends):
    blocks = [a.reshape(NDP, -1, a.shape[1]) for a in addends]

    def part(k, r):
        return jnp.concatenate([rows_of(b, k, r) for b in blocks], axis=1)

    to_far = shift(part(2, 1).astype(BF16), "x", 1, NX)
    back_far = shift(part(3, 1).astype(BF16), "x", -1, NX)
    to_own = shift(part(2, 0).astype(BF16), "x", -1, NX)
    on_far = shift((part(1, 1) + to_far.astype(F32)).astype(BF16), "x", 1, NX)
    far = part(0, 1) + on_far.astype(F32) + back_far.astype(F32)
    across = shift(far.astype(BF16), "zh", 1, NZH)
    on_own = shift(part(1, 0).astype(BF16), "x", 1, NX)
    back_own = shift((part(3, 0) + to_own.astype(F32)).astype(BF16), "x", -1, NX)
    own = part(0, 0) + on_own.astype(F32) + back_own.astype(F32)
    return own + across.astype(F32)


def gather_over_dp(own, late):
    rows, width = own.shape
    cut = (rows // 2 + 7) // 8 * 8
    full = jnp.zeros((NDP, rows, width), BF16)

    def put(full, piece, k, r, row=0):
        return lax.dynamic_update_slice(full, piece[None], (chunk_index(k, r), row, 0))

    other = shift(own, "zh", 1, NZH)
    full = put(full, own, 0, 0)
    for r, mine in ((0, own), (1, other)):
        if r:
            full = put(full, mine, 0, 1)
        before = shift(mine, "x", 1, NX)
        after = shift(mine, "x", -1, NX)
        if r:
            before, after, late = lax.optimization_barrier((before, after, late))
        top = shift(before[:cut], "x", 1, NX)
        low = shift(after[cut:], "x", -1, NX)
        full = put(full, before, 3, r)
        full = put(full, after, 1, r)
        full = put(full, top, 2, r)
        full = put(full, low, 2, r, cut)
    return full, late


def rows_of(blocks, k, r):
    return lax.dynamic_index_in_dim(blocks, chunk_index(k, r), 0, keepdims=False)


def all_near(value):
    return [value] + [shift(value, "zl", k, NZL) for k in range(1, NZL)]


def sum_near(blocks):
    total = blocks[0]
    for k in range(1, NZL):
        total = total + shift(blocks[k].astype(BF16), "zl", -k, NZL).astype(F32)
    return total


def to_owner(rows):
    return lax.all_to_all(rows, YC, 0, 0, tiled=True)


def gather_by_swap(rows):
    return to_owner(jnp.broadcast_to(rows[None], (NYC, *rows.shape))).reshape(-1, rows.shape[1])


def body(
    tokens,
    route_ids,
    route_weights,
    w_gate,
    w_up,
    w_down,
    shared_gate,
    shared_up,
    shared_down,
    cotangent,
):
    tok_rows, top_count = route_ids.shape
    features = tokens.shape[1]
    hidden_exp = w_gate.shape[2]
    hidden_sh = shared_gate.shape[1]
    experts = NYC * NZL
    average = tok_rows * top_count // experts
    capacity = average + max(average // 12, 2)
    span = NZL * capacity
    all_rows = NZL * tok_rows
    zl = lax.axis_index("zl")

    routes = jnp.concatenate([route_ids.T.astype(F32), route_weights.T], axis=0)
    routes_all = jnp.concatenate(all_near(routes), axis=1)
    pair = jnp.concatenate([cotangent, tokens], axis=1)
    pair_all = jnp.concatenate(all_near(pair), axis=0)
    cot_all, tok_all = pair_all[:, :features], pair_all[:, features:]

    ids = routes_all[:top_count].astype(jnp.int32)
    weights = routes_all[top_count:]
    place = jnp.arange(NYC, dtype=jnp.int32)
    expert = (place // NC) * (NZL * NC) + zl * NC + place % NC
    hit = ids[None] == expert[:, None, None]
    member = jnp.sum(hit.astype(F32), axis=1)
    weight = jnp.sum(jnp.where(hit, weights[None], 0.0), axis=1)
    earlier = (
        lax.broadcasted_iota(jnp.int32, (tok_rows, tok_rows), 0)
        < lax.broadcasted_iota(jnp.int32, (tok_rows, tok_rows), 1)
    ).astype(BF16)
    before = dot(member.astype(BF16).reshape(NYC * NZL, tok_rows), earlier)
    before = before.reshape(NYC, all_rows).astype(jnp.int32)
    block = jnp.arange(all_rows, dtype=jnp.int32) // tok_rows
    slot = jnp.where(member > 0, before + block[None] * capacity, -1)
    chosen = slot[:, None, :] == lax.broadcasted_iota(jnp.int32, (NYC, span, all_rows), 1)
    weight_high = weight.astype(BF16)
    weight_low = (weight - weight_high.astype(F32)).astype(BF16)
    zero = jnp.zeros((), BF16)
    pick = chosen.astype(BF16).reshape(NYC * span, all_rows)
    pick_high = jnp.where(chosen, weight_high[:, None, :], zero).reshape(NYC * span, all_rows)
    pick_low = jnp.where(chosen, weight_low[:, None, :], zero).reshape(NYC * span, all_rows)

    grad_rows = (dot(pick_high, cot_all) + dot(pick_low, cot_all)).astype(BF16)
    grad_in = to_owner(grad_rows.reshape(NYC, span, features))
    send_rows = dot(pick, tok_all).astype(BF16)
    arrived = to_owner(send_rows.reshape(NYC, span, features))

    joined = jnp.concatenate([w_gate[0], w_up[0]], axis=1)
    down = w_down[0]

    part_sh = hidden_sh // NZL
    piece = part_sh // NY
    rows_sh = shared_gate.shape[0]

    def by_zl(w):
        w = w.reshape(rows_sh, NY, NZL, piece).transpose(2, 0, 1, 3)
        return w.reshape(NZL, rows_sh, part_sh)

    both = jnp.concatenate([by_zl(shared_gate), by_zl(shared_up)], axis=2)
    both = lax.all_to_all(both, "zl", 0, 0, tiled=True).reshape(NZL * rows_sh, 2 * part_sh)
    both = gather_by_swap(both)
    sh_down = gather_by_swap(shared_down)
    feature = jnp.arange(features, dtype=jnp.int32)
    f_row, f_c = feature % rows_sh, feature // rows_sh % NC
    f_zl, f_y = feature // (rows_sh * NC) % NZL, feature // (rows_sh * NC * NZL)
    came = ((f_y * NC + f_c) * NZL + f_zl) * rows_sh + f_row
    order = (
        came[:, None] == lax.broadcasted_iota(jnp.int32, (features, features), 1)
    ).astype(BF16)
    sh_join = dot(order, both).astype(BF16)

    sh_own = reduce_over_dp(
        jnp.concatenate([dot(tok_all, sh_join), dot(cot_all, sh_down, 1, 1)], axis=1)
    )
    sh_gate_pre = sh_own[:, :part_sh]
    sh_up_pre = sh_own[:, part_sh : 2 * part_sh]
    sh_hidden = activate(sh_gate_pre, sh_up_pre)
    sh_pregrad = activation_grad(sh_gate_pre, sh_up_pre, sh_own[:, 2 * part_sh :])
    sh_full = lax.all_gather(
        jnp.concatenate([sh_hidden, *sh_pregrad], axis=1).astype(BF16), DP, axis=0, tiled=True
    )
    slots = NYC * span
    arrived = arrived.reshape(slots, features)
    grad_in = grad_in.reshape(slots, features)
    own = reduce_over_dp(dot(arrived, joined), dot(grad_in, down, 1, 1))
    gate_pre, up_pre = own[:, :hidden_exp], own[:, hidden_exp : 2 * hidden_exp]
    hidden_own = activate(gate_pre, up_pre)
    pregrad_own = activation_grad(gate_pre, up_pre, own[:, 2 * hidden_exp :])
    full, sh_full = gather_over_dp(
        jnp.concatenate([hidden_own, *pregrad_own], axis=1).astype(BF16), sh_full
    )
    full = full.reshape(slots, 3 * hidden_exp)
    hidden_full = full[:, :hidden_exp]
    pregrad_full = full[:, hidden_exp:]

    sh_hidden_full = sh_full[:, :part_sh]
    sh_pregrad_full = sh_full[:, part_sh:]

    expert_out = dot(hidden_full, down).astype(BF16)
    returned = to_owner(expert_out.reshape(NYC, span, features)).reshape(slots, features)
    out_part = (
        dot(sh_hidden_full, sh_down)
        + dot(pick_high, returned, 0, 0)
        + dot(pick_low, returned, 0, 0)
    )
    output = sum_near(list(out_part.reshape(NZL, tok_rows, features))).astype(BF16)

    input_grad = dot(pregrad_full, joined, 1, 1).astype(BF16)
    grad_back = to_owner(input_grad.reshape(NYC, span, features)).reshape(slots, features)
    tok_part = dot(sh_pregrad_full, sh_join, 1, 1) + dot(pick, grad_back, 0, 0)
    d_tokens = sum_near(list(tok_part.reshape(NZL, tok_rows, features))).astype(BF16)

    grad_down = dot(hidden_full, grad_in, 0, 0).astype(BF16)[None]
    grad_join = dot(arrived, pregrad_full, 0, 0).astype(BF16)
    grad_gate = grad_join[None, :, :hidden_exp]
    grad_up = grad_join[None, :, hidden_exp:]

    sh_grad = dot(tok_all, sh_pregrad_full, 0, 0).astype(BF16)
    sh_grad = dot(order, sh_grad, 0, 0).astype(BF16)
    sh_grad = to_owner(sh_grad.reshape(NYC, NZL * rows_sh, 2 * part_sh))
    sh_grad = jnp.sum(sh_grad.astype(F32), axis=0).astype(BF16)
    sh_grad = lax.all_to_all(
        sh_grad.reshape(NZL, rows_sh, 2 * part_sh), "zl", 0, 0, tiled=True
    )

    def from_zl(g):
        g = g.reshape(NZL, rows_sh, NY, piece).transpose(1, 2, 0, 3)
        return g.reshape(rows_sh, hidden_sh)

    grad_shared_gate = from_zl(sh_grad[:, :, :part_sh])
    grad_shared_up = from_zl(sh_grad[:, :, part_sh:])
    sh_down_grad = dot(sh_hidden_full, cot_all, 0, 0).astype(BF16)
    sh_down_grad = to_owner(sh_down_grad.reshape(NYC, part_sh // NYC, features))
    grad_shared_down = jnp.sum(sh_down_grad.astype(F32), axis=0).astype(BF16)
    return (
        output,
        d_tokens,
        grad_gate,
        grad_up,
        grad_down,
        grad_shared_gate,
        grad_shared_up,
        grad_shared_down,
    )


def solution(mesh):
    parts = Mesh(
        mesh.devices.reshape(NX, NZH, NY, NZL, NC), ("x", "zh", "y", "zl", "c")
    )
    dp, expert = ("x", "zh"), ("y", "zl", "c")
    in_specs = (
        P(expert, dp),
        P(expert, None),
        P(expert, None),
        P(expert, dp, None),
        P(expert, dp, None),
        P(expert, None, dp),
        P(dp + expert, None),
        P(dp + expert, None),
        P(expert, dp),
        P(expert, dp),
    )
    out_specs = (
        P(expert, dp),
        P(expert, dp),
        P(expert, dp, None),
        P(expert, dp, None),
        P(expert, None, dp),
        P(dp + expert, None),
        P(dp + expert, None),
        P(expert, dp),
    )
    return jax.shard_map(
        body, mesh=parts, in_specs=in_specs, out_specs=out_specs, check_vma=False
    )
```

```python
import jax
import jax.numpy as jnp
from jax import lax
from jax.sharding import Mesh, PartitionSpec as P

BF16 = jnp.bfloat16
F32 = jnp.float32
NX, NZH, NY, NZL, NC = 4, 2, 4, 4, 2
DP = ("x", "zh")
YC = ("y", "c")
NDP = NX * NZH
NYC = NY * NC


def shift(value, axis, by, size):
    return lax.ppermute(value, axis, [(i, (i + by) % size) for i in range(size)])


def dot(left, right, left_dim=1, right_dim=0):
    return lax.dot_general(
        left, right, (((left_dim,), (right_dim,)), ((), ())), preferred_element_type=F32
    )


def activate(gate, up):
    return gate * jax.nn.sigmoid(gate) * up


def activation_grad(gate, up, hidden_grad):
    s = jax.nn.sigmoid(gate)
    return (
        hidden_grad * up * s * (1.0 + gate * (1.0 - s)),
        hidden_grad * (gate * s),
    )


def chunk_index(k, r):
    return ((lax.axis_index("x") + k) % NX) * NZH + (lax.axis_index("zh") + r) % NZH


def reduce_over_dp(*addends, direct=False, due=()):
    blocks = [a.reshape(NDP, -1, a.shape[1]) for a in addends]

    def part(k, r):
        return jnp.stack([rows_of(b, k, r) for b in blocks])

    if direct:
        sides = []
        for r in (1, 0):
            side = part(0, r)
            for k in range(1, NX):
                side = side + shift(part(k, r).astype(BF16), "x", k, NX).astype(F32)
            sides.append(side)
        return sides[1] + shift(sides[0].astype(BF16), "zh", 1, NZH).astype(F32), due
    to_far = shift(part(2, 1).astype(BF16), "x", 1, NX)
    back_far = shift(part(3, 1).astype(BF16), "x", -1, NX)
    to_own = shift(part(2, 0).astype(BF16), "x", -1, NX)
    on_far = shift((part(1, 1) + to_far.astype(F32)).astype(BF16), "x", 1, NX)
    far = part(0, 1) + on_far.astype(F32) + back_far.astype(F32)
    across = shift(far.astype(BF16), "zh", 1, NZH)
    on_own = shift(part(1, 0).astype(BF16), "x", 1, NX)
    back_own = shift((part(3, 0) + to_own.astype(F32)).astype(BF16), "x", -1, NX)
    own = part(0, 0) + on_own.astype(F32) + back_own.astype(F32)
    across, due = lax.optimization_barrier((across, due))
    return own + across.astype(F32), due


def gather_over_dp(own, direct=False, due=()):
    parts, rows, width = own.shape
    cut = (rows // 2 + 7) // 8 * 8
    full = jnp.zeros((parts, NDP, rows, width), BF16)

    def put(full, piece, k, r, row=0):
        return lax.dynamic_update_slice(full, piece[:, None], (0, chunk_index(k, r), row, 0))

    other = shift(own, "zh", 1, NZH)
    full = put(full, own, 0, 0)
    for r, mine in ((0, own), (1, other)):
        if r:
            full = put(full, mine, 0, 1)
        if direct:
            for k in range(1, NX):
                full = put(full, shift(mine, "x", -k, NX), k, r)
            continue
        before = shift(mine, "x", 1, NX)
        after = shift(mine, "x", -1, NX)
        if r:
            before, after, due = lax.optimization_barrier((before, after, due))
        top = shift(before[:, :cut], "x", 1, NX)
        low = shift(after[:, cut:], "x", -1, NX)
        full = put(full, before, 3, r)
        full = put(full, after, 1, r)
        full = put(full, top, 2, r)
        full = put(full, low, 2, r, cut)
    return full, due


def rows_of(blocks, k, r):
    return lax.dynamic_index_in_dim(blocks, chunk_index(k, r), 0, keepdims=False)


def all_near(value):
    return [value] + [shift(value, "zl", k, NZL) for k in range(1, NZL)]


def sum_near(blocks):
    total = blocks[0]
    for k in range(1, NZL):
        total = total + shift(blocks[k].astype(BF16), "zl", -k, NZL).astype(F32)
    return total


def to_owner(rows):
    return lax.all_to_all(rows, YC, 0, 0, tiled=True)


def gather_by_swap(rows):
    return to_owner(jnp.broadcast_to(rows[None], (NYC, *rows.shape))).reshape(-1, rows.shape[1])


def body(
    tokens,
    route_ids,
    route_weights,
    w_gate,
    w_up,
    w_down,
    shared_gate,
    shared_up,
    shared_down,
    cotangent,
):
    tok_rows, top_count = route_ids.shape
    features = tokens.shape[1]
    hidden_exp = w_gate.shape[2]
    hidden_sh = shared_gate.shape[1]
    experts = NYC * NZL
    average = tok_rows * top_count // experts
    capacity = average + max(average // 12, 2)
    span = NZL * capacity
    all_rows = NZL * tok_rows
    zl = lax.axis_index("zl")

    routes = jnp.concatenate([route_ids.T.astype(F32), route_weights.T], axis=0)
    routes_all = lax.all_gather(routes, "zl", axis=0)
    routes_all, cotangent, tokens = lax.optimization_barrier((routes_all, cotangent, tokens))
    near = (zl - jnp.arange(NZL, dtype=jnp.int32)) % NZL
    routes_all = jnp.concatenate(
        [lax.dynamic_index_in_dim(routes_all, near[k], 0, keepdims=False) for k in range(NZL)], axis=1
    )
    cot_near = all_near(cotangent)

    part_sh = hidden_sh // NZL
    piece = part_sh // NY
    rows_sh = shared_gate.shape[0]

    def by_zl(w):
        w = w.reshape(rows_sh, NY, NZL, piece).transpose(2, 0, 1, 3)
        return w.reshape(NZL, rows_sh, part_sh)

    both = jnp.concatenate([by_zl(shared_gate), by_zl(shared_up)], axis=2)
    both = lax.all_to_all(both, "zl", 0, 0, tiled=True).reshape(NZL * rows_sh, 2 * part_sh)
    sh_down = lax.all_gather(shared_down, YC, axis=0, tiled=True)
    both, cot_near, tokens = lax.optimization_barrier((both, cot_near, tokens))
    both = gather_by_swap(both)
    cot_all = jnp.concatenate(cot_near, axis=0)
    tok_all = jnp.concatenate(all_near(tokens), axis=0)

    ids = routes_all[:top_count].astype(jnp.int32)
    weights = routes_all[top_count:]
    place = jnp.arange(NYC, dtype=jnp.int32)
    expert = (place // NC) * (NZL * NC) + zl * NC + place % NC
    hit = ids[None] == expert[:, None, None]
    member = jnp.sum(hit.astype(F32), axis=1)
    weight = jnp.sum(jnp.where(hit, weights[None], 0.0), axis=1)
    earlier = (
        lax.broadcasted_iota(jnp.int32, (tok_rows, tok_rows), 0)
        < lax.broadcasted_iota(jnp.int32, (tok_rows, tok_rows), 1)
    ).astype(BF16)
    before = dot(member.astype(BF16).reshape(NYC * NZL, tok_rows), earlier)
    before = before.reshape(NYC, all_rows).astype(jnp.int32)
    block = jnp.arange(all_rows, dtype=jnp.int32) // tok_rows
    slot = jnp.where(member > 0, before + block[None] * capacity, -1)
    chosen = slot[:, None, :] == lax.broadcasted_iota(jnp.int32, (NYC, span, all_rows), 1)
    weight_high = weight.astype(BF16)
    weight_low = (weight - weight_high.astype(F32)).astype(BF16)
    zero = jnp.zeros((), BF16)
    pick = chosen.astype(BF16).reshape(NYC * span, all_rows)
    pick_high = jnp.where(chosen, weight_high[:, None, :], zero).reshape(NYC * span, all_rows)
    pick_low = jnp.where(chosen, weight_low[:, None, :], zero).reshape(NYC * span, all_rows)

    grad_rows = (dot(pick_high, cot_all) + dot(pick_low, cot_all)).astype(BF16)
    grad_in = to_owner(grad_rows.reshape(NYC, span, features))
    send_rows = dot(pick, tok_all).astype(BF16)
    arrived = to_owner(send_rows.reshape(NYC, span, features))

    gate_w, up_w, down = w_gate[0], w_up[0], w_down[0]

    feature = jnp.arange(features, dtype=jnp.int32)
    f_row, f_c = feature % rows_sh, feature // rows_sh % NC
    f_zl, f_y = feature // (rows_sh * NC) % NZL, feature // (rows_sh * NC * NZL)
    came = ((f_y * NC + f_c) * NZL + f_zl) * rows_sh + f_row
    order = (
        came[:, None] == lax.broadcasted_iota(jnp.int32, (features, features), 1)
    ).astype(BF16)
    sh_join = dot(order, both).astype(BF16)

    sh_own = reduce_over_dp(
        jnp.concatenate([dot(tok_all, sh_join), dot(cot_all, sh_down, 1, 1)], axis=1), direct=True
    )[0][0]
    sh_gate_pre = sh_own[:, :part_sh]
    sh_up_pre = sh_own[:, part_sh : 2 * part_sh]
    sh_hidden = activate(sh_gate_pre, sh_up_pre)
    sh_pregrad = activation_grad(sh_gate_pre, sh_up_pre, sh_own[:, 2 * part_sh :])
    sh_full = gather_over_dp(
        jnp.concatenate([sh_hidden, *sh_pregrad], axis=1).astype(BF16)[None], direct=True
    )[0].reshape(all_rows, 3 * part_sh)
    slots = NYC * span
    arrived = arrived.reshape(slots, features)
    grad_in = grad_in.reshape(slots, features)
    addends = (dot(arrived, gate_w), dot(arrived, up_w), dot(grad_in, down, 1, 1))
    addends, sh_full = lax.optimization_barrier((addends, sh_full))
    sh_hidden_full = sh_full[:, :part_sh]
    sh_pregrad_full = sh_full[:, part_sh:]
    sh_grad = dot(tok_all, sh_pregrad_full, 0, 0).astype(BF16)
    sh_grad = dot(order, sh_grad, 0, 0).astype(BF16)
    sh_grad = to_owner(sh_grad.reshape(NYC, NZL * rows_sh, 2 * part_sh))
    sh_down_grad = dot(sh_hidden_full, cot_all, 0, 0).astype(BF16)
    sh_down_grad = to_owner(sh_down_grad.reshape(NYC, part_sh // NYC, features))
    own, (sh_grad, sh_down_grad) = reduce_over_dp(*addends, due=(sh_grad, sh_down_grad))
    gate_pre, up_pre, hidden_grad = own
    hidden_own = activate(gate_pre, up_pre)
    pregrad_own = activation_grad(gate_pre, up_pre, hidden_grad)
    sh_grad = jnp.sum(sh_grad.astype(F32), axis=0).astype(BF16)
    sh_grad = lax.all_to_all(
        sh_grad.reshape(NZL, rows_sh, 2 * part_sh), "zl", 0, 0, tiled=True
    )
    full, sh_grad = gather_over_dp(
        jnp.stack([hidden_own, *pregrad_own]).astype(BF16), due=sh_grad
    )
    full = full.reshape(3, slots, hidden_exp)
    hidden_full, gate_full, up_full = full

    expert_out = dot(hidden_full, down).astype(BF16)
    returned = to_owner(expert_out.reshape(NYC, span, features)).reshape(slots, features)
    out_part = (
        dot(sh_hidden_full, sh_down)
        + dot(pick_high, returned, 0, 0)
        + dot(pick_low, returned, 0, 0)
    )
    out_part, full_late, arrived_late, grad_late = lax.optimization_barrier(
        (out_part, full, arrived, grad_in)
    )
    hidden_late, gate_late, up_late = full_late
    output = sum_near(list(out_part.reshape(NZL, tok_rows, features))).astype(BF16)

    input_grad = (dot(gate_full, gate_w, 1, 1) + dot(up_full, up_w, 1, 1)).astype(BF16)
    grad_back = to_owner(input_grad.reshape(NYC, span, features)).reshape(slots, features)
    output, grad_back = lax.optimization_barrier((output, grad_back))
    tok_part = dot(sh_pregrad_full, sh_join, 1, 1) + dot(pick, grad_back, 0, 0)
    d_tokens = sum_near(list(tok_part.reshape(NZL, tok_rows, features))).astype(BF16)

    grad_down = dot(hidden_late, grad_late, 0, 0).astype(BF16)[None]
    grad_gate = dot(arrived_late, gate_late, 0, 0).astype(BF16)[None]
    grad_up = dot(arrived_late, up_late, 0, 0).astype(BF16)[None]

    def from_zl(g):
        g = g.reshape(NZL, rows_sh, NY, piece).transpose(1, 2, 0, 3)
        return g.reshape(rows_sh, hidden_sh)

    grad_shared_gate = from_zl(sh_grad[:, :, :part_sh])
    grad_shared_up = from_zl(sh_grad[:, :, part_sh:])
    grad_shared_down = jnp.sum(sh_down_grad.astype(F32), axis=0).astype(BF16)
    return (
        output,
        d_tokens,
        grad_gate,
        grad_up,
        grad_down,
        grad_shared_gate,
        grad_shared_up,
        grad_shared_down,
    )


def solution(mesh):
    parts = Mesh(
        mesh.devices.reshape(NX, NZH, NY, NZL, NC), ("x", "zh", "y", "zl", "c")
    )
    dp, expert = ("x", "zh"), ("y", "zl", "c")
    in_specs = (
        P(expert, dp),
        P(expert, None),
        P(expert, None),
        P(expert, dp, None),
        P(expert, dp, None),
        P(expert, None, dp),
        P(dp + expert, None),
        P(dp + expert, None),
        P(expert, dp),
        P(expert, dp),
    )
    out_specs = (
        P(expert, dp),
        P(expert, dp),
        P(expert, dp, None),
        P(expert, dp, None),
        P(expert, None, dp),
        P(dp + expert, None),
        P(dp + expert, None),
        P(expert, dp),
    )
    return jax.shard_map(
        body, mesh=parts, in_specs=in_specs, out_specs=out_specs, check_vma=False
    )
```

```python
import jax
import jax.numpy as jnp
from jax import lax
from jax.sharding import Mesh, PartitionSpec as P

BF16 = jnp.bfloat16
F32 = jnp.float32
NX, NZH, NY, NZL, NC = 4, 2, 4, 4, 2
DP = ("x", "zh")
YC = ("y", "c")
NDP = NX * NZH
NYC = NY * NC


def shift(value, axis, by, size):
    return lax.ppermute(value, axis, [(i, (i + by) % size) for i in range(size)])


def dot(left, right, left_dim=1, right_dim=0):
    return lax.dot_general(
        left, right, (((left_dim,), (right_dim,)), ((), ())), preferred_element_type=F32
    )


def activate(gate, up):
    return gate * jax.nn.sigmoid(gate) * up


def activation_grad(gate, up, hidden_grad):
    s = jax.nn.sigmoid(gate)
    return (
        hidden_grad * up * s * (1.0 + gate * (1.0 - s)),
        hidden_grad * (gate * s),
    )


def chunk_index(k, r):
    return ((lax.axis_index("x") + k) % NX) * NZH + (lax.axis_index("zh") + r) % NZH


def reduce_over_dp(*addends, direct=False, due=()):
    blocks = [a.reshape(NDP, -1, a.shape[1]) for a in addends]

    def part(k, r):
        return jnp.stack([rows_of(b, k, r) for b in blocks])

    if direct:
        sides = []
        for r in (1, 0):
            side = part(0, r)
            for k in range(1, NX):
                side = side + shift(part(k, r).astype(BF16), "x", k, NX).astype(F32)
            sides.append(side)
        return sides[1] + shift(sides[0].astype(BF16), "zh", 1, NZH).astype(F32), due
    to_far = shift(part(2, 1).astype(BF16), "x", 1, NX)
    back_far = shift(part(3, 1).astype(BF16), "x", -1, NX)
    to_own = shift(part(2, 0).astype(BF16), "x", -1, NX)
    on_far = shift((part(1, 1) + to_far.astype(F32)).astype(BF16), "x", 1, NX)
    far = part(0, 1) + on_far.astype(F32) + back_far.astype(F32)
    across = shift(far.astype(BF16), "zh", 1, NZH)
    on_own = shift(part(1, 0).astype(BF16), "x", 1, NX)
    back_own = shift((part(3, 0) + to_own.astype(F32)).astype(BF16), "x", -1, NX)
    own = part(0, 0) + on_own.astype(F32) + back_own.astype(F32)
    across, due = lax.optimization_barrier((across, due))
    return own + across.astype(F32), due


def gather_over_dp(own, sizes, direct=False, due=()):
    parts, rows, width = own.shape
    cut = (rows // 2 + 7) // 8 * 8
    full = [jnp.zeros((size, NDP, rows, width), BF16) for size in sizes]

    def put(full, piece, k, r, row=0):
        out, at = [], 0
        for whole, size in zip(full, sizes):
            part = piece[at : at + size, None]
            out.append(lax.dynamic_update_slice(whole, part, (0, chunk_index(k, r), row, 0)))
            at += size
        return out

    other = shift(own, "zh", 1, NZH)
    full = put(full, own, 0, 0)
    for r, mine in ((0, own), (1, other)):
        if r:
            full = put(full, mine, 0, 1)
        if direct:
            for k in range(1, NX):
                full = put(full, shift(mine, "x", -k, NX), k, r)
            continue
        before = shift(mine, "x", 1, NX)
        after = shift(mine, "x", -1, NX)
        if r:
            before, after, due = lax.optimization_barrier((before, after, due))
        top = shift(before[:, :cut], "x", 1, NX)
        low = shift(after[:, cut:], "x", -1, NX)
        full = put(full, before, 3, r)
        full = put(full, after, 1, r)
        full = put(full, top, 2, r)
        full = put(full, low, 2, r, cut)
    return full, due


def rows_of(blocks, k, r):
    return lax.dynamic_index_in_dim(blocks, chunk_index(k, r), 0, keepdims=False)


def all_near(value):
    return [value] + [shift(value, "zl", k, NZL) for k in range(1, NZL)]


def send_near(blocks):
    return [shift(blocks[k].astype(BF16), "zl", -k, NZL) for k in range(1, NZL)]


def add_near(blocks, sent):
    return sum((b.astype(F32) for b in sent), blocks[0]).astype(BF16)


def to_owner(rows):
    return lax.all_to_all(rows, YC, 0, 0, tiled=True)


def gather_by_swap(rows):
    return to_owner(jnp.broadcast_to(rows[None], (NYC, *rows.shape))).reshape(-1, rows.shape[1])


def body(
    tokens,
    route_ids,
    route_weights,
    w_gate,
    w_up,
    w_down,
    shared_gate,
    shared_up,
    shared_down,
    cotangent,
):
    tok_rows, top_count = route_ids.shape
    features = tokens.shape[1]
    hidden_exp = w_gate.shape[2]
    hidden_sh = shared_gate.shape[1]
    experts = NYC * NZL
    average = tok_rows * top_count // experts
    capacity = average + max(average // 12, 2)
    span = NZL * capacity
    all_rows = NZL * tok_rows
    zl = lax.axis_index("zl")

    routes = jnp.concatenate([route_ids.T.astype(F32), route_weights.T], axis=0)
    routes_all = jnp.concatenate(all_near(routes), axis=1)
    routes_all, tokens = lax.optimization_barrier((routes_all, tokens))
    cot_near = all_near(cotangent)

    part_sh = hidden_sh // NZL
    piece = part_sh // NY
    rows_sh = shared_gate.shape[0]

    def by_zl(w):
        w = w.reshape(rows_sh, NY, NZL, piece).transpose(2, 0, 1, 3)
        return w.reshape(NZL, rows_sh, part_sh)

    both = jnp.concatenate([by_zl(shared_gate), by_zl(shared_up)], axis=2)
    both = lax.all_to_all(both, "zl", 0, 0, tiled=True).reshape(NZL * rows_sh, 2 * part_sh)
    sh_down = lax.all_gather(shared_down, YC, axis=0, tiled=True)
    both, cot_near = lax.optimization_barrier((both, cot_near))
    both = gather_by_swap(both)
    cot_all = jnp.concatenate(cot_near, axis=0)
    both, tok_near = lax.optimization_barrier((both, all_near(tokens)))
    tok_all = jnp.concatenate(tok_near, axis=0)

    ids = routes_all[:top_count].astype(jnp.int32)
    weights = routes_all[top_count:]
    place = jnp.arange(NYC, dtype=jnp.int32)
    expert = (place // NC) * (NZL * NC) + zl * NC + place % NC
    hit = ids[None] == expert[:, None, None]
    member = jnp.sum(hit.astype(F32), axis=1)
    weight = jnp.sum(jnp.where(hit, weights[None], 0.0), axis=1)
    earlier = (
        lax.broadcasted_iota(jnp.int32, (tok_rows, tok_rows), 0)
        < lax.broadcasted_iota(jnp.int32, (tok_rows, tok_rows), 1)
    ).astype(BF16)
    before = dot(member.astype(BF16).reshape(NYC * NZL, tok_rows), earlier)
    before = before.reshape(NYC, all_rows).astype(jnp.int32)
    block = jnp.arange(all_rows, dtype=jnp.int32) // tok_rows
    slot = jnp.where(member > 0, before + block[None] * capacity, -1)
    chosen = slot[:, None, :] == lax.broadcasted_iota(jnp.int32, (NYC, span, all_rows), 1)
    weight_high = weight.astype(BF16)
    weight_low = (weight - weight_high.astype(F32)).astype(BF16)
    zero = jnp.zeros((), BF16)
    pick = chosen.astype(BF16).reshape(NYC * span, all_rows)
    pick_high = jnp.where(chosen, weight_high[:, None, :], zero).reshape(NYC * span, all_rows)
    pick_low = jnp.where(chosen, weight_low[:, None, :], zero).reshape(NYC * span, all_rows)

    grad_rows = (dot(pick_high, cot_all) + dot(pick_low, cot_all)).astype(BF16)
    grad_in = to_owner(grad_rows.reshape(NYC, span, features))
    send_rows = dot(pick, tok_all).astype(BF16)
    arrived = to_owner(send_rows.reshape(NYC, span, features))

    gate_w, up_w, down = w_gate[0], w_up[0], w_down[0]

    feature = jnp.arange(features, dtype=jnp.int32)
    f_row, f_c = feature % rows_sh, feature // rows_sh % NC
    f_zl, f_y = feature // (rows_sh * NC) % NZL, feature // (rows_sh * NC * NZL)
    came = ((f_y * NC + f_c) * NZL + f_zl) * rows_sh + f_row
    order = (
        came[:, None] == lax.broadcasted_iota(jnp.int32, (features, features), 1)
    ).astype(BF16)
    sh_join = dot(order, both).astype(BF16)

    sh_own = reduce_over_dp(
        jnp.concatenate([dot(tok_all, sh_join), dot(cot_all, sh_down, 1, 1)], axis=1), direct=True
    )[0][0]
    sh_gate_pre = sh_own[:, :part_sh]
    sh_up_pre = sh_own[:, part_sh : 2 * part_sh]
    sh_hidden = activate(sh_gate_pre, sh_up_pre)
    sh_pregrad = activation_grad(sh_gate_pre, sh_up_pre, sh_own[:, 2 * part_sh :])
    sh_full = gather_over_dp(
        jnp.concatenate([sh_hidden, *sh_pregrad], axis=1).astype(BF16)[None], (1,), direct=True
    )[0][0].reshape(all_rows, 3 * part_sh)
    slots = NYC * span
    arrived = arrived.reshape(slots, features)
    grad_in = grad_in.reshape(slots, features)
    addends = (dot(arrived, gate_w), dot(arrived, up_w), dot(grad_in, down, 1, 1))
    addends, sh_full = lax.optimization_barrier((addends, sh_full))
    sh_hidden_full = sh_full[:, :part_sh]
    sh_pregrad_full = sh_full[:, part_sh:]
    sh_grad = dot(tok_all, sh_pregrad_full, 0, 0).astype(BF16)
    sh_grad = dot(order, sh_grad, 0, 0).astype(BF16)
    sh_grad = to_owner(sh_grad.reshape(NYC, NZL * rows_sh, 2 * part_sh))
    sh_down_grad = dot(sh_hidden_full, cot_all, 0, 0).astype(BF16)
    sh_down_grad = to_owner(sh_down_grad.reshape(NYC, part_sh // NYC, features))
    own, (sh_grad, sh_down_grad) = reduce_over_dp(*addends, due=(sh_grad, sh_down_grad))
    gate_pre, up_pre, hidden_grad = own
    hidden_own = activate(gate_pre, up_pre)
    pregrad_own = activation_grad(gate_pre, up_pre, hidden_grad)
    sh_grad = jnp.sum(sh_grad.astype(F32), axis=0).astype(BF16)
    sh_grad = lax.all_to_all(
        sh_grad.reshape(NZL, rows_sh, 2 * part_sh), "zl", 0, 0, tiled=True
    )
    (hidden_full, slope_full), sh_grad = gather_over_dp(
        jnp.stack([hidden_own, *pregrad_own]).astype(BF16), (1, 2), due=sh_grad
    )
    hidden_full = hidden_full.reshape(slots, hidden_exp)
    slope_full = slope_full.reshape(2, slots, hidden_exp)
    gate_full, up_full = slope_full

    expert_out = dot(hidden_full, down).astype(BF16)
    returned = to_owner(expert_out.reshape(NYC, span, features)).reshape(slots, features)
    out_part = (
        dot(sh_hidden_full, sh_down)
        + dot(pick_high, returned, 0, 0)
        + dot(pick_low, returned, 0, 0)
    )
    out_part, hidden_late, slope_late, arrived_late, grad_late = lax.optimization_barrier(
        (out_part, hidden_full, slope_full, arrived, grad_in)
    )
    gate_late, up_late = slope_late
    out_blocks = list(out_part.reshape(NZL, tok_rows, features))
    out_sent = send_near(out_blocks)

    input_grad = (dot(gate_full, gate_w, 1, 1) + dot(up_full, up_w, 1, 1)).astype(BF16)
    grad_back = to_owner(input_grad.reshape(NYC, span, features)).reshape(slots, features)
    out_sent[0], grad_back = lax.optimization_barrier((out_sent[0], grad_back))
    output = add_near(out_blocks, out_sent)
    tok_part = dot(sh_pregrad_full, sh_join, 1, 1) + dot(pick, grad_back, 0, 0)
    tok_blocks = list(tok_part.reshape(NZL, tok_rows, features))
    d_tokens = add_near(tok_blocks, send_near(tok_blocks))

    grad_down = dot(hidden_late, grad_late, 0, 0).astype(BF16)[None]
    grad_gate = dot(arrived_late, gate_late, 0, 0).astype(BF16)[None]
    grad_up = dot(arrived_late, up_late, 0, 0).astype(BF16)[None]

    def from_zl(g):
        g = g.reshape(NZL, rows_sh, NY, piece).transpose(1, 2, 0, 3)
        return g.reshape(rows_sh, hidden_sh)

    grad_shared_gate = from_zl(sh_grad[:, :, :part_sh])
    grad_shared_up = from_zl(sh_grad[:, :, part_sh:])
    grad_shared_down = jnp.sum(sh_down_grad.astype(F32), axis=0).astype(BF16)
    return (
        output,
        d_tokens,
        grad_gate,
        grad_up,
        grad_down,
        grad_shared_gate,
        grad_shared_up,
        grad_shared_down,
    )


def solution(mesh):
    parts = Mesh(
        mesh.devices.reshape(NX, NZH, NY, NZL, NC), ("x", "zh", "y", "zl", "c")
    )
    dp, expert = ("x", "zh"), ("y", "zl", "c")
    in_specs = (
        P(expert, dp),
        P(expert, None),
        P(expert, None),
        P(expert, dp, None),
        P(expert, dp, None),
        P(expert, None, dp),
        P(dp + expert, None),
        P(dp + expert, None),
        P(expert, dp),
        P(expert, dp),
    )
    out_specs = (
        P(expert, dp),
        P(expert, dp),
        P(expert, dp, None),
        P(expert, dp, None),
        P(expert, None, dp),
        P(dp + expert, None),
        P(dp + expert, None),
        P(expert, dp),
    )
    return jax.shard_map(
        body, mesh=parts, in_specs=in_specs, out_specs=out_specs, check_vma=False
    )
```

```python
import jax
import jax.numpy as jnp
from jax import lax
from jax.sharding import Mesh, PartitionSpec as P

BF16 = jnp.bfloat16
F32 = jnp.float32
NX, NZH, NY, NZL, NC = 4, 2, 4, 4, 2
DP = ("x", "zh")
YC = ("y", "c")
NDP = NX * NZH
NYC = NY * NC


def shift(value, axis, by, size):
    return lax.ppermute(value, axis, [(i, (i + by) % size) for i in range(size)])


def dot(left, right, left_dim=1, right_dim=0):
    return lax.dot_general(
        left, right, (((left_dim,), (right_dim,)), ((), ())), preferred_element_type=F32
    )


def activate(gate, up):
    return gate * jax.nn.sigmoid(gate) * up


def activation_grad(gate, up, hidden_grad):
    s = jax.nn.sigmoid(gate)
    return (
        hidden_grad * up * s * (1.0 + gate * (1.0 - s)),
        hidden_grad * (gate * s),
    )


def chunk_index(k, r):
    return ((lax.axis_index("x") + k) % NX) * NZH + (lax.axis_index("zh") + r) % NZH


def reduce_over_dp(*addends, direct=False, due=()):
    blocks = [a.reshape(NDP, -1, a.shape[1]) for a in addends]

    def part(k, r):
        return jnp.stack([rows_of(b, k, r) for b in blocks])

    if direct:
        sides = []
        for r in (1, 0):
            side = part(0, r)
            for k in range(1, NX):
                side = side + shift(part(k, r).astype(BF16), "x", k, NX).astype(F32)
            sides.append(side)
        return sides[1] + shift(sides[0].astype(BF16), "zh", 1, NZH).astype(F32), due
    to_far = shift(part(2, 1).astype(BF16), "x", 1, NX)
    back_far = shift(part(3, 1).astype(BF16), "x", -1, NX)
    to_far, back_far, send = lax.optimization_barrier((to_far, back_far, part(2, 0).astype(BF16)))
    to_own = shift(send, "x", -1, NX)
    on_far = shift((part(1, 1) + to_far.astype(F32)).astype(BF16), "x", 1, NX)
    on_far, to_own, send = lax.optimization_barrier((on_far, to_own, part(1, 0).astype(BF16)))
    far = part(0, 1) + on_far.astype(F32) + back_far.astype(F32)
    across = shift(far.astype(BF16), "zh", 1, NZH)
    on_own = shift(send, "x", 1, NX)
    back_own = shift((part(3, 0) + to_own.astype(F32)).astype(BF16), "x", -1, NX)
    own = part(0, 0) + on_own.astype(F32) + back_own.astype(F32)
    across, due = lax.optimization_barrier((across, due))
    return own + across.astype(F32), due


def gather_over_dp(own, sizes, direct=False, due=()):
    parts, rows, width = own.shape
    cut = (rows // 2 + 7) // 8 * 8
    full = [jnp.zeros((size, NDP, rows, width), BF16) for size in sizes]

    def put(full, piece, k, r, row=0):
        out, at = [], 0
        for whole, size in zip(full, sizes):
            part = piece[at : at + size, None]
            out.append(lax.dynamic_update_slice(whole, part, (0, chunk_index(k, r), row, 0)))
            at += size
        return out

    other = shift(own, "zh", 1, NZH)
    full = put(full, own, 0, 0)
    for r, mine in ((0, own), (1, other)):
        if r:
            full = put(full, mine, 0, 1)
        if direct:
            if r:
                mine, due = lax.optimization_barrier((mine, due))
            for k in range(1, NX):
                full = put(full, shift(mine, "x", -k, NX), k, r)
            continue
        before = shift(mine, "x", 1, NX)
        after = shift(mine, "x", -1, NX)
        if r:
            before, after, due = lax.optimization_barrier((before, after, due))
        top = shift(before[:, :cut], "x", 1, NX)
        low = shift(after[:, cut:], "x", -1, NX)
        full = put(full, before, 3, r)
        full = put(full, after, 1, r)
        full = put(full, top, 2, r)
        full = put(full, low, 2, r, cut)
    return full, due


def rows_of(blocks, k, r):
    return lax.dynamic_index_in_dim(blocks, chunk_index(k, r), 0, keepdims=False)


def all_near(value):
    return [value] + [shift(value, "zl", k, NZL) for k in range(1, NZL)]


def send_near(blocks):
    return [shift(blocks[k].astype(BF16), "zl", -k, NZL) for k in range(1, NZL)]


def add_near(blocks, sent):
    return sum((b.astype(F32) for b in sent), blocks[0]).astype(BF16)


def to_owner(rows):
    return lax.all_to_all(rows, YC, 0, 0, tiled=True)


def gather_by_swap(rows):
    return to_owner(jnp.broadcast_to(rows[None], (NYC, *rows.shape))).reshape(-1, rows.shape[1])


def body(
    tokens,
    route_ids,
    route_weights,
    w_gate,
    w_up,
    w_down,
    shared_gate,
    shared_up,
    shared_down,
    cotangent,
):
    tok_rows, top_count = route_ids.shape
    features = tokens.shape[1]
    hidden_exp = w_gate.shape[2]
    hidden_sh = shared_gate.shape[1]
    experts = NYC * NZL
    average = tok_rows * top_count // experts
    capacity = average + max(average // 12, 2)
    span = NZL * capacity
    all_rows = NZL * tok_rows
    zl = lax.axis_index("zl")

    pair_near = all_near(jnp.concatenate([cotangent, tokens], axis=1))

    part_sh = hidden_sh // NZL
    piece = part_sh // NY
    rows_sh = shared_gate.shape[0]

    def by_zl(w):
        w = w.reshape(rows_sh, NY, NZL, piece).transpose(2, 0, 1, 3)
        return w.reshape(NZL, rows_sh, part_sh)

    high = route_weights.astype(BF16)
    low = (route_weights - high.astype(F32)).astype(BF16)
    spare = 8 - top_count
    routes = [
        jnp.pad(r.T, ((0, spare), (0, 0))) for r in (route_ids.astype(BF16), high, low)
    ]
    routes = jnp.concatenate(routes, axis=1)
    routes = jnp.pad(routes, ((0, 0), (0, 2 * part_sh - routes.shape[1])))
    both = jnp.concatenate([by_zl(shared_gate), by_zl(shared_up)], axis=2)
    both = jnp.concatenate([jnp.broadcast_to(routes[None], (NZL, *routes.shape)), both], axis=1)
    both = lax.all_to_all(both, "zl", 0, 0, tiled=True)
    routes_all = both[:, :top_count, : 3 * tok_rows]
    both = both[:, 8:].reshape(NZL * rows_sh, 2 * part_sh)
    sh_down = lax.all_gather(shared_down, YC, axis=0, tiled=True)
    both = gather_by_swap(both)
    both, pair_near = lax.optimization_barrier((both, pair_near))
    pair_all = jnp.concatenate(pair_near, axis=0)
    cot_all, tok_all = pair_all[:, :features], pair_all[:, features:]

    ids, high, low = [
        jnp.concatenate(
            [
                lax.dynamic_index_in_dim(
                    routes_all[:, :, i * tok_rows : (i + 1) * tok_rows],
                    (zl - k) % NZL,
                    0,
                    keepdims=False,
                )
                for k in range(NZL)
            ],
            axis=1,
        )
        for i in range(3)
    ]
    ids = ids.astype(jnp.int32)
    place = jnp.arange(NYC, dtype=jnp.int32)
    expert = (place // NC) * (NZL * NC) + zl * NC + place % NC
    hit = ids[None] == expert[:, None, None]
    member = jnp.sum(hit.astype(F32), axis=1)
    weight_high, weight_low = [
        jnp.sum(jnp.where(hit, w.astype(F32)[None], 0.0), axis=1).astype(BF16) for w in (high, low)
    ]
    earlier = (
        lax.broadcasted_iota(jnp.int32, (tok_rows, tok_rows), 0)
        < lax.broadcasted_iota(jnp.int32, (tok_rows, tok_rows), 1)
    ).astype(BF16)
    before = dot(member.astype(BF16).reshape(NYC * NZL, tok_rows), earlier)
    before = before.reshape(NYC, all_rows).astype(jnp.int32)
    block = jnp.arange(all_rows, dtype=jnp.int32) // tok_rows
    slot = jnp.where(member > 0, before + block[None] * capacity, -1)
    chosen = slot[:, None, :] == lax.broadcasted_iota(jnp.int32, (NYC, span, all_rows), 1)
    zero = jnp.zeros((), BF16)
    pick = chosen.astype(BF16).reshape(NYC * span, all_rows)
    pick_high = jnp.where(chosen, weight_high[:, None, :], zero).reshape(NYC * span, all_rows)
    pick_low = jnp.where(chosen, weight_low[:, None, :], zero).reshape(NYC * span, all_rows)

    send_rows = dot(pick, tok_all).astype(BF16)
    send_rows, both = lax.optimization_barrier((send_rows, both))
    arrived = to_owner(send_rows.reshape(NYC, span, features))
    grad_rows = (dot(pick_high, cot_all) + dot(pick_low, cot_all)).astype(BF16)
    grad_in = to_owner(grad_rows.reshape(NYC, span, features))

    gate_w, up_w, down = w_gate[0], w_up[0], w_down[0]

    feature = jnp.arange(features, dtype=jnp.int32)
    f_row, f_c = feature % rows_sh, feature // rows_sh % NC
    f_zl, f_y = feature // (rows_sh * NC) % NZL, feature // (rows_sh * NC * NZL)
    came = ((f_y * NC + f_c) * NZL + f_zl) * rows_sh + f_row
    order = (
        came[:, None] == lax.broadcasted_iota(jnp.int32, (features, features), 1)
    ).astype(BF16)
    sh_join = dot(order, both).astype(BF16)

    sh_own = reduce_over_dp(
        jnp.concatenate([dot(tok_all, sh_join), dot(cot_all, sh_down, 1, 1)], axis=1), direct=True
    )[0][0]
    sh_own, arrived = lax.optimization_barrier((sh_own, arrived))
    sh_gate_pre = sh_own[:, :part_sh]
    sh_up_pre = sh_own[:, part_sh : 2 * part_sh]
    sh_hidden = activate(sh_gate_pre, sh_up_pre)
    sh_pregrad = activation_grad(sh_gate_pre, sh_up_pre, sh_own[:, 2 * part_sh :])
    sh_full, grad_in = gather_over_dp(
        jnp.concatenate([sh_hidden, *sh_pregrad], axis=1).astype(BF16)[None],
        (1,),
        direct=True,
        due=grad_in,
    )
    sh_full = sh_full[0].reshape(all_rows, 3 * part_sh)
    slots = NYC * span
    arrived = arrived.reshape(slots, features)
    grad_in = grad_in.reshape(slots, features)
    addends = (dot(arrived, gate_w), dot(arrived, up_w), dot(grad_in, down, 1, 1))
    addends, sh_full = lax.optimization_barrier((addends, sh_full))
    sh_hidden_full = sh_full[:, :part_sh]
    sh_pregrad_full = sh_full[:, part_sh:]
    sh_grad = dot(tok_all, sh_pregrad_full, 0, 0).astype(BF16)
    sh_grad = dot(order, sh_grad, 0, 0).astype(BF16)
    sh_grad = to_owner(sh_grad.reshape(NYC, NZL * rows_sh, 2 * part_sh))
    sh_down_grad = dot(sh_hidden_full, cot_all, 0, 0).astype(BF16)
    sh_down_grad = to_owner(sh_down_grad.reshape(NYC, part_sh // NYC, features))
    own, (sh_grad, sh_down_grad) = reduce_over_dp(*addends, due=(sh_grad, sh_down_grad))
    gate_pre, up_pre, hidden_grad = own
    hidden_own = activate(gate_pre, up_pre)
    pregrad_own = activation_grad(gate_pre, up_pre, hidden_grad)
    sh_grad = jnp.sum(sh_grad.astype(F32), axis=0).astype(BF16)
    sh_grad = lax.all_to_all(
        sh_grad.reshape(NZL, rows_sh, 2 * part_sh), "zl", 0, 0, tiled=True
    )
    (hidden_full, slope_full), sh_grad = gather_over_dp(
        jnp.stack([hidden_own, *pregrad_own]).astype(BF16), (1, 2), due=sh_grad
    )
    hidden_full = hidden_full.reshape(slots, hidden_exp)
    slope_full = slope_full.reshape(2, slots, hidden_exp)
    gate_full, up_full = slope_full

    expert_out = dot(hidden_full, down).astype(BF16)
    expert_out, hidden_late, grad_late = lax.optimization_barrier((expert_out, hidden_full, grad_in))
    returned = to_owner(expert_out.reshape(NYC, span, features)).reshape(slots, features)
    out_part = (
        dot(sh_hidden_full, sh_down)
        + dot(pick_high, returned, 0, 0)
        + dot(pick_low, returned, 0, 0)
    )
    out_blocks = list(out_part.reshape(NZL, tok_rows, features))
    out_sent = send_near(out_blocks)

    input_grad = (dot(gate_full, gate_w, 1, 1) + dot(up_full, up_w, 1, 1)).astype(BF16)
    grad_back = to_owner(input_grad.reshape(NYC, span, features)).reshape(slots, features)
    out_sent[0], grad_back = lax.optimization_barrier((out_sent[0], grad_back))
    output = add_near(out_blocks, out_sent)
    tok_part = dot(sh_pregrad_full, sh_join, 1, 1) + dot(pick, grad_back, 0, 0)
    tok_blocks = list(tok_part.reshape(NZL, tok_rows, features))
    tok_sent = send_near(tok_blocks)
    tok_sent[0], slope_late, arrived_late = lax.optimization_barrier(
        (tok_sent[0], slope_full, arrived)
    )
    gate_late, up_late = slope_late
    d_tokens = add_near(tok_blocks, tok_sent)

    grad_down = dot(hidden_late, grad_late, 0, 0).astype(BF16)[None]
    grad_gate = dot(arrived_late, gate_late, 0, 0).astype(BF16)[None]
    grad_up = dot(arrived_late, up_late, 0, 0).astype(BF16)[None]

    def from_zl(g):
        g = g.reshape(NZL, rows_sh, NY, piece).transpose(1, 2, 0, 3)
        return g.reshape(rows_sh, hidden_sh)

    grad_shared_gate = from_zl(sh_grad[:, :, :part_sh])
    grad_shared_up = from_zl(sh_grad[:, :, part_sh:])
    grad_shared_down = jnp.sum(sh_down_grad.astype(F32), axis=0).astype(BF16)
    return (
        output,
        d_tokens,
        grad_gate,
        grad_up,
        grad_down,
        grad_shared_gate,
        grad_shared_up,
        grad_shared_down,
    )


def solution(mesh):
    parts = Mesh(
        mesh.devices.reshape(NX, NZH, NY, NZL, NC), ("x", "zh", "y", "zl", "c")
    )
    dp, expert = ("x", "zh"), ("y", "zl", "c")
    in_specs = (
        P(expert, dp),
        P(expert, None),
        P(expert, None),
        P(expert, dp, None),
        P(expert, dp, None),
        P(expert, None, dp),
        P(dp + expert, None),
        P(dp + expert, None),
        P(expert, dp),
        P(expert, dp),
    )
    out_specs = (
        P(expert, dp),
        P(expert, dp),
        P(expert, dp, None),
        P(expert, dp, None),
        P(expert, None, dp),
        P(dp + expert, None),
        P(dp + expert, None),
        P(expert, dp),
    )
    return jax.shard_map(
        body, mesh=parts, in_specs=in_specs, out_specs=out_specs, check_vma=False
    )
```

```python
import jax
import jax.numpy as jnp
from jax import lax
from jax.sharding import Mesh, PartitionSpec as P

BF16 = jnp.bfloat16
F32 = jnp.float32
NX, NZH, NY, NZL, NC = 4, 2, 4, 4, 2
DP = ("x", "zh")
YC = ("y", "c")
NDP = NX * NZH
NYC = NY * NC


def shift(value, axis, by, size):
    return lax.ppermute(value, axis, [(i, (i + by) % size) for i in range(size)])


def dot(left, right, left_dim=1, right_dim=0):
    return lax.dot_general(
        left, right, (((left_dim,), (right_dim,)), ((), ())), preferred_element_type=F32
    )


def activate(gate, up):
    return gate * jax.nn.sigmoid(gate) * up


def activation_grad(gate, up, hidden_grad):
    s = jax.nn.sigmoid(gate)
    return (
        hidden_grad * up * s * (1.0 + gate * (1.0 - s)),
        hidden_grad * (gate * s),
    )


def chunk_index(k, r):
    return ((lax.axis_index("x") + k) % NX) * NZH + (lax.axis_index("zh") + r) % NZH


def reduce_over_dp(*addends, direct=False, due=()):
    blocks = [a.reshape(NDP, -1, a.shape[1]) for a in addends]

    def part(k, r):
        return jnp.stack([rows_of(b, k, r) for b in blocks])

    if direct:
        sides = []
        for r in (1, 0):
            side = part(0, r)
            for k in range(1, NX):
                side = side + shift(part(k, r).astype(BF16), "x", k, NX).astype(F32)
            sides.append(side)
        return sides[1] + shift(sides[0].astype(BF16), "zh", 1, NZH).astype(F32), due
    to_far = shift(part(2, 1).astype(BF16), "x", 1, NX)
    back_far = shift(part(3, 1).astype(BF16), "x", -1, NX)
    to_far, back_far, send = lax.optimization_barrier((to_far, back_far, part(2, 0).astype(BF16)))
    to_own = shift(send, "x", -1, NX)
    on_far = shift((part(1, 1) + to_far.astype(F32)).astype(BF16), "x", 1, NX)
    on_far, to_own, send = lax.optimization_barrier((on_far, to_own, part(1, 0).astype(BF16)))
    far = part(0, 1) + on_far.astype(F32) + back_far.astype(F32)
    across = shift(far.astype(BF16), "zh", 1, NZH)
    on_own = shift(send, "x", 1, NX)
    back_own = shift((part(3, 0) + to_own.astype(F32)).astype(BF16), "x", -1, NX)
    own = part(0, 0) + on_own.astype(F32) + back_own.astype(F32)
    across, due = lax.optimization_barrier((across, due))
    return own + across.astype(F32), due


def gather_over_dp(own, sizes, direct=False, due=(), then=None):
    parts, rows, width = own.shape
    cut = (rows // 2 + 7) // 8 * 8
    full = [jnp.zeros((size, NDP, rows, width), BF16) for size in sizes]

    def put(full, piece, k, r, row=0):
        out, at = [], 0
        for whole, size in zip(full, sizes):
            part = piece[at : at + size, None]
            out.append(lax.dynamic_update_slice(whole, part, (0, chunk_index(k, r), row, 0)))
            at += size
        return out

    other = shift(own, "zh", 1, NZH)
    full = put(full, own, 0, 0)
    for r, mine in ((0, own), (1, other)):
        if r:
            full = put(full, mine, 0, 1)
        if direct:
            if r:
                mine, due = lax.optimization_barrier((mine, due))
            came = [shift(mine, "x", -k, NX) for k in range(1, NX)]
            if r and then:
                came, due = lax.optimization_barrier((came, then(due)))
            for k in range(1, NX):
                full = put(full, came[k - 1], k, r)
            continue
        before = shift(mine, "x", 1, NX)
        after = shift(mine, "x", -1, NX)
        if r:
            before, after, due = lax.optimization_barrier((before, after, due))
        top = shift(before[:, :cut], "x", 1, NX)
        low = shift(after[:, cut:], "x", -1, NX)
        full = put(full, before, 3, r)
        full = put(full, after, 1, r)
        full = put(full, top, 2, r)
        full = put(full, low, 2, r, cut)
    return full, due


def rows_of(blocks, k, r):
    return lax.dynamic_index_in_dim(blocks, chunk_index(k, r), 0, keepdims=False)


def all_near(value):
    return [value] + [shift(value, "zl", k, NZL) for k in range(1, NZL)]


def send_near(blocks):
    return [shift(blocks[k].astype(BF16), "zl", -k, NZL) for k in range(1, NZL)]


def add_near(blocks, sent):
    return sum((b.astype(F32) for b in sent), blocks[0]).astype(BF16)


def to_owner(rows):
    return lax.all_to_all(rows, YC, 0, 0, tiled=True)


def gather_by_swap(rows):
    return to_owner(jnp.broadcast_to(rows[None], (NYC, *rows.shape))).reshape(-1, rows.shape[1])


def body(
    tokens,
    route_ids,
    route_weights,
    w_gate,
    w_up,
    w_down,
    shared_gate,
    shared_up,
    shared_down,
    cotangent,
):
    tok_rows, top_count = route_ids.shape
    features = tokens.shape[1]
    hidden_exp = w_gate.shape[2]
    hidden_sh = shared_gate.shape[1]
    experts = NYC * NZL
    average = tok_rows * top_count // experts
    capacity = average + max(average // 12, 2)
    span = NZL * capacity
    all_rows = NZL * tok_rows
    zl = lax.axis_index("zl")

    cot_near = all_near(cotangent)

    part_sh = hidden_sh // NZL
    piece = part_sh // NY
    rows_sh = shared_gate.shape[0]

    def by_zl(w):
        w = w.reshape(rows_sh, NY, NZL, piece).transpose(2, 0, 1, 3)
        return w.reshape(NZL, rows_sh, part_sh)

    high = route_weights.astype(BF16)
    low = (route_weights - high.astype(F32)).astype(BF16)
    spare = 8 - top_count
    routes = [
        jnp.pad(r.T, ((0, spare), (0, 0))) for r in (route_ids.astype(BF16), high, low)
    ]
    routes = jnp.concatenate(routes, axis=1)
    routes = jnp.pad(routes, ((0, 0), (0, 2 * part_sh - routes.shape[1])))
    both = jnp.concatenate([by_zl(shared_gate), by_zl(shared_up)], axis=2)
    both = jnp.concatenate([jnp.broadcast_to(routes[None], (NZL, *routes.shape)), both], axis=1)
    both = lax.all_to_all(both, "zl", 0, 0, tiled=True)
    routes_all = both[:, :top_count, : 3 * tok_rows]
    both = both[:, 8:].reshape(NZL * rows_sh, 2 * part_sh)
    sh_down = lax.all_gather(shared_down, YC, axis=0, tiled=True)
    both, tokens = lax.optimization_barrier((both, tokens))
    both = gather_by_swap(both)
    cot_all = jnp.concatenate(cot_near, axis=0)
    both, tok_near = lax.optimization_barrier((both, all_near(tokens)))
    tok_all = jnp.concatenate(tok_near, axis=0)

    ids, high, low = [
        jnp.concatenate(
            [
                lax.dynamic_index_in_dim(
                    routes_all[:, :, i * tok_rows : (i + 1) * tok_rows],
                    (zl - k) % NZL,
                    0,
                    keepdims=False,
                )
                for k in range(NZL)
            ],
            axis=1,
        )
        for i in range(3)
    ]
    ids = ids.astype(jnp.int32)
    place = jnp.arange(NYC, dtype=jnp.int32)
    expert = (place // NC) * (NZL * NC) + zl * NC + place % NC
    hit = ids[None] == expert[:, None, None]
    member = jnp.sum(hit.astype(F32), axis=1)
    weight_high, weight_low = [
        jnp.sum(jnp.where(hit, w.astype(F32)[None], 0.0), axis=1).astype(BF16) for w in (high, low)
    ]
    earlier = (
        lax.broadcasted_iota(jnp.int32, (tok_rows, tok_rows), 0)
        < lax.broadcasted_iota(jnp.int32, (tok_rows, tok_rows), 1)
    ).astype(BF16)
    before = dot(member.astype(BF16).reshape(NYC * NZL, tok_rows), earlier)
    before = before.reshape(NYC, all_rows).astype(jnp.int32)
    block = jnp.arange(all_rows, dtype=jnp.int32) // tok_rows
    slot = jnp.where(member > 0, before + block[None] * capacity, -1)
    chosen = slot[:, None, :] == lax.broadcasted_iota(jnp.int32, (NYC, span, all_rows), 1)
    zero = jnp.zeros((), BF16)
    pick = chosen.astype(BF16).reshape(NYC * span, all_rows)
    pick_high = jnp.where(chosen, weight_high[:, None, :], zero).reshape(NYC * span, all_rows)
    pick_low = jnp.where(chosen, weight_low[:, None, :], zero).reshape(NYC * span, all_rows)

    grad_rows = (dot(pick_high, cot_all) + dot(pick_low, cot_all)).astype(BF16)
    grad_rows, both = lax.optimization_barrier((grad_rows, both))
    grad_in = to_owner(grad_rows.reshape(NYC, span, features))
    send_rows = dot(pick, tok_all).astype(BF16)
    arrived = to_owner(send_rows.reshape(NYC, span, features))

    gate_w, up_w, down = w_gate[0], w_up[0], w_down[0]

    feature = jnp.arange(features, dtype=jnp.int32)
    f_row, f_c = feature % rows_sh, feature // rows_sh % NC
    f_zl, f_y = feature // (rows_sh * NC) % NZL, feature // (rows_sh * NC * NZL)
    came = ((f_y * NC + f_c) * NZL + f_zl) * rows_sh + f_row
    order = (
        came[:, None] == lax.broadcasted_iota(jnp.int32, (features, features), 1)
    ).astype(BF16)
    sh_join = dot(order, both).astype(BF16)

    sh_own = reduce_over_dp(
        jnp.concatenate([dot(tok_all, sh_join), dot(cot_all, sh_down, 1, 1)], axis=1), direct=True
    )[0][0]
    sh_own, grad_in = lax.optimization_barrier((sh_own, grad_in))
    sh_gate_pre = sh_own[:, :part_sh]
    sh_up_pre = sh_own[:, part_sh : 2 * part_sh]
    sh_hidden = activate(sh_gate_pre, sh_up_pre)
    sh_pregrad = activation_grad(sh_gate_pre, sh_up_pre, sh_own[:, 2 * part_sh :])
    sh_full, addends = gather_over_dp(
        jnp.concatenate([sh_hidden, *sh_pregrad], axis=1).astype(BF16)[None],
        (1,),
        direct=True,
        due=(arrived, grad_in),
        then=lambda due: (
            dot(due[0].reshape(-1, features), gate_w),
            dot(due[0].reshape(-1, features), up_w),
            dot(due[1].reshape(-1, features), down, 1, 1),
        ),
    )
    sh_full = sh_full[0].reshape(all_rows, 3 * part_sh)
    slots = NYC * span
    arrived = arrived.reshape(slots, features)
    grad_in = grad_in.reshape(slots, features)
    sh_hidden_full = sh_full[:, :part_sh]
    sh_pregrad_full = sh_full[:, part_sh:]
    sh_grad = dot(tok_all, sh_pregrad_full, 0, 0).astype(BF16)
    sh_grad = dot(order, sh_grad, 0, 0).astype(BF16)
    sh_grad = to_owner(sh_grad.reshape(NYC, NZL * rows_sh, 2 * part_sh))
    sh_down_grad = dot(sh_hidden_full, cot_all, 0, 0).astype(BF16)
    sh_down_grad = to_owner(sh_down_grad.reshape(NYC, part_sh // NYC, features))
    own, (sh_grad, sh_down_grad) = reduce_over_dp(*addends, due=(sh_grad, sh_down_grad))
    gate_pre, up_pre, hidden_grad = own
    hidden_own = activate(gate_pre, up_pre)
    pregrad_own = activation_grad(gate_pre, up_pre, hidden_grad)
    sh_grad = jnp.sum(sh_grad.astype(F32), axis=0).astype(BF16)
    sh_grad = lax.all_to_all(
        sh_grad.reshape(NZL, rows_sh, 2 * part_sh), "zl", 0, 0, tiled=True
    )
    (hidden_full, slope_full), sh_grad = gather_over_dp(
        jnp.stack([hidden_own, *pregrad_own]).astype(BF16), (1, 2), due=sh_grad
    )
    hidden_full = hidden_full.reshape(slots, hidden_exp)
    slope_full = slope_full.reshape(2, slots, hidden_exp)
    gate_full, up_full = slope_full

    expert_out = dot(hidden_full, down).astype(BF16)
    expert_out, hidden_late, grad_late = lax.optimization_barrier((expert_out, hidden_full, grad_in))
    grad_down = dot(hidden_late, grad_late, 0, 0).astype(BF16)[None]
    returned = to_owner(expert_out.reshape(NYC, span, features)).reshape(slots, features)
    out_part = (
        dot(sh_hidden_full, sh_down)
        + dot(pick_high, returned, 0, 0)
        + dot(pick_low, returned, 0, 0)
    )
    out_blocks = list(out_part.reshape(NZL, tok_rows, features))
    out_sent = send_near(out_blocks)

    input_grad = (dot(gate_full, gate_w, 1, 1) + dot(up_full, up_w, 1, 1)).astype(BF16)
    input_grad, grad_down = lax.optimization_barrier((input_grad, grad_down))
    grad_back = to_owner(input_grad.reshape(NYC, span, features)).reshape(slots, features)
    out_part, slope_late, arrived_late = lax.optimization_barrier((out_part, slope_full, arrived))
    grad_gate = dot(arrived_late, slope_late[0], 0, 0).astype(BF16)[None]
    out_sent[0], grad_gate, grad_back = lax.optimization_barrier((out_sent[0], grad_gate, grad_back))
    output = add_near(out_blocks, out_sent)
    tok_part = dot(sh_pregrad_full, sh_join, 1, 1) + dot(pick, grad_back, 0, 0)
    tok_blocks = list(tok_part.reshape(NZL, tok_rows, features))
    tok_sent = send_near(tok_blocks)
    tok_sent[0], slope_late, arrived_late = lax.optimization_barrier(
        (tok_sent[0], slope_full, arrived)
    )
    d_tokens = add_near(tok_blocks, tok_sent)

    grad_up = dot(arrived_late, slope_late[1], 0, 0).astype(BF16)[None]

    def from_zl(g):
        g = g.reshape(NZL, rows_sh, NY, piece).transpose(1, 2, 0, 3)
        return g.reshape(rows_sh, hidden_sh)

    grad_shared_gate = from_zl(sh_grad[:, :, :part_sh])
    grad_shared_up = from_zl(sh_grad[:, :, part_sh:])
    grad_shared_down = jnp.sum(sh_down_grad.astype(F32), axis=0).astype(BF16)
    return (
        output,
        d_tokens,
        grad_gate,
        grad_up,
        grad_down,
        grad_shared_gate,
        grad_shared_up,
        grad_shared_down,
    )


def solution(mesh):
    parts = Mesh(
        mesh.devices.reshape(NX, NZH, NY, NZL, NC), ("x", "zh", "y", "zl", "c")
    )
    dp, expert = ("x", "zh"), ("y", "zl", "c")
    in_specs = (
        P(expert, dp),
        P(expert, None),
        P(expert, None),
        P(expert, dp, None),
        P(expert, dp, None),
        P(expert, None, dp),
        P(dp + expert, None),
        P(dp + expert, None),
        P(expert, dp),
        P(expert, dp),
    )
    out_specs = (
        P(expert, dp),
        P(expert, dp),
        P(expert, dp, None),
        P(expert, dp, None),
        P(expert, None, dp),
        P(dp + expert, None),
        P(dp + expert, None),
        P(expert, dp),
    )
    return jax.shard_map(
        body, mesh=parts, in_specs=in_specs, out_specs=out_specs, check_vma=False
    )
```

```python
import jax
import jax.numpy as jnp
from jax import lax
from jax.sharding import Mesh, PartitionSpec as P

BF16 = jnp.bfloat16
F32 = jnp.float32
NX, NZH, NY, NZL, NC = 4, 2, 4, 4, 2
DP = ("x", "zh")
YC = ("y", "c")
NDP = NX * NZH
NYC = NY * NC


def shift(value, axis, by, size):
    return lax.ppermute(value, axis, [(i, (i + by) % size) for i in range(size)])


def dot(left, right, left_dim=1, right_dim=0):
    return lax.dot_general(
        left, right, (((left_dim,), (right_dim,)), ((), ())), preferred_element_type=F32
    )


def activate(gate, up):
    return gate * jax.nn.sigmoid(gate) * up


def activation_grad(gate, up, hidden_grad):
    s = jax.nn.sigmoid(gate)
    return (
        hidden_grad * up * s * (1.0 + gate * (1.0 - s)),
        hidden_grad * (gate * s),
    )


def chunk_index(k, r):
    return ((lax.axis_index("x") + k) % NX) * NZH + (lax.axis_index("zh") + r) % NZH


def reduce_over_dp(*addends, direct=False, due=()):
    blocks = [a.reshape(NDP, -1, a.shape[1]) for a in addends]

    def part(k, r):
        return jnp.stack([rows_of(b, k, r) for b in blocks])

    if direct:
        sides = []
        for r in (1, 0):
            side = part(0, r)
            came = [shift(part(k, r).astype(BF16), "x", k, NX) for k in range(1, NX)]
            if r:
                came, due = lax.optimization_barrier((came, due))
            for piece in came:
                side = side + piece.astype(F32)
            sides.append(side)
        return sides[1] + shift(sides[0].astype(BF16), "zh", 1, NZH).astype(F32), due
    to_far = shift(part(2, 1).astype(BF16), "x", 1, NX)
    back_far = shift(part(3, 1).astype(BF16), "x", -1, NX)
    to_far, back_far, send = lax.optimization_barrier((to_far, back_far, part(2, 0).astype(BF16)))
    to_own = shift(send, "x", -1, NX)
    on_far = shift((part(1, 1) + to_far.astype(F32)).astype(BF16), "x", 1, NX)
    on_far, to_own, send = lax.optimization_barrier((on_far, to_own, part(1, 0).astype(BF16)))
    far = part(0, 1) + on_far.astype(F32) + back_far.astype(F32)
    across = shift(far.astype(BF16), "zh", 1, NZH)
    on_own = shift(send, "x", 1, NX)
    back_own = shift((part(3, 0) + to_own.astype(F32)).astype(BF16), "x", -1, NX)
    own = part(0, 0) + on_own.astype(F32) + back_own.astype(F32)
    across, due = lax.optimization_barrier((across, due))
    return own + across.astype(F32), due


def gather_over_dp(own, sizes, direct=False, due=(), then=None):
    parts, rows, width = own.shape
    cut = (rows // 2 + 7) // 8 * 8
    full = [jnp.zeros((size, NDP, rows, width), BF16) for size in sizes]

    def put(full, piece, k, r, row=0):
        out, at = [], 0
        for whole, size in zip(full, sizes):
            part = piece[at : at + size, None]
            out.append(lax.dynamic_update_slice(whole, part, (0, chunk_index(k, r), row, 0)))
            at += size
        return out

    other = shift(own, "zh", 1, NZH)
    full = put(full, own, 0, 0)
    for r, mine in ((0, own), (1, other)):
        if r:
            full = put(full, mine, 0, 1)
        if direct:
            if r:
                mine, due = lax.optimization_barrier((mine, due))
            came = [shift(mine, "x", -k, NX) for k in range(1, NX)]
            if r and then:
                came, due = lax.optimization_barrier((came, then(due)))
            for k in range(1, NX):
                full = put(full, came[k - 1], k, r)
            continue
        before = shift(mine, "x", 1, NX)
        after = shift(mine, "x", -1, NX)
        if r:
            before, after, due = lax.optimization_barrier((before, after, due))
        top = shift(before[:, :cut], "x", 1, NX)
        low = shift(after[:, cut:], "x", -1, NX)
        full = put(full, before, 3, r)
        full = put(full, after, 1, r)
        full = put(full, top, 2, r)
        full = put(full, low, 2, r, cut)
    return full, due


def rows_of(blocks, k, r):
    return lax.dynamic_index_in_dim(blocks, chunk_index(k, r), 0, keepdims=False)


def all_near(value):
    return [value] + [shift(value, "zl", k, NZL) for k in range(1, NZL)]


def send_near(blocks):
    return [shift(blocks[k].astype(BF16), "zl", -k, NZL) for k in range(1, NZL)]


def add_near(blocks, sent):
    return sum((b.astype(F32) for b in sent), blocks[0]).astype(BF16)


def to_owner(rows):
    return lax.all_to_all(rows, YC, 0, 0, tiled=True)


def gather_by_swap(rows):
    return to_owner(jnp.broadcast_to(rows[None], (NYC, *rows.shape))).reshape(-1, rows.shape[1])


def body(
    tokens,
    route_ids,
    route_weights,
    w_gate,
    w_up,
    w_down,
    shared_gate,
    shared_up,
    shared_down,
    cotangent,
):
    tok_rows, top_count = route_ids.shape
    features = tokens.shape[1]
    hidden_exp = w_gate.shape[2]
    hidden_sh = shared_gate.shape[1]
    experts = NYC * NZL
    average = tok_rows * top_count // experts
    capacity = average + max(average // 12, 2)
    span = NZL * capacity
    all_rows = NZL * tok_rows
    zl = lax.axis_index("zl")

    cot_near = all_near(cotangent)

    part_sh = hidden_sh // NZL
    piece = part_sh // NY
    rows_sh = shared_gate.shape[0]

    def by_zl(w):
        w = w.reshape(rows_sh, NY, NZL, piece).transpose(2, 0, 1, 3)
        return w.reshape(NZL, rows_sh, part_sh)

    high = route_weights.astype(BF16)
    low = (route_weights - high.astype(F32)).astype(BF16)
    spare = 8 - top_count
    routes = [
        jnp.pad(r.T, ((0, spare), (0, 0))) for r in (route_ids.astype(BF16), high, low)
    ]
    routes = jnp.concatenate(routes, axis=1)
    routes = jnp.pad(routes, ((0, 0), (0, 2 * part_sh - routes.shape[1])))
    both = jnp.concatenate([by_zl(shared_gate), by_zl(shared_up)], axis=2)
    both = jnp.concatenate([jnp.broadcast_to(routes[None], (NZL, *routes.shape)), both], axis=1)
    both = lax.all_to_all(both, "zl", 0, 0, tiled=True)
    routes_all = both[:, :top_count, : 3 * tok_rows]
    both = both[:, 8:].reshape(NZL * rows_sh, 2 * part_sh)
    sh_down = lax.all_gather(shared_down, YC, axis=0, tiled=True)
    both, tokens = lax.optimization_barrier((both, tokens))
    both = gather_by_swap(both)
    cot_all = jnp.concatenate(cot_near, axis=0)
    both, tok_near = lax.optimization_barrier((both, all_near(tokens)))
    tok_all = jnp.concatenate(tok_near, axis=0)

    ids, high, low = [
        jnp.concatenate(
            [
                lax.dynamic_index_in_dim(
                    routes_all[:, :, i * tok_rows : (i + 1) * tok_rows],
                    (zl - k) % NZL,
                    0,
                    keepdims=False,
                )
                for k in range(NZL)
            ],
            axis=1,
        )
        for i in range(3)
    ]
    ids = ids.astype(jnp.int32)
    place = jnp.arange(NYC, dtype=jnp.int32)
    expert = (place // NC) * (NZL * NC) + zl * NC + place % NC
    hit = ids[None] == expert[:, None, None]
    member = jnp.sum(hit.astype(F32), axis=1)
    weight_high, weight_low = [
        jnp.sum(jnp.where(hit, w.astype(F32)[None], 0.0), axis=1).astype(BF16) for w in (high, low)
    ]
    earlier = (
        lax.broadcasted_iota(jnp.int32, (tok_rows, tok_rows), 0)
        < lax.broadcasted_iota(jnp.int32, (tok_rows, tok_rows), 1)
    ).astype(BF16)
    before = dot(member.astype(BF16).reshape(NYC * NZL, tok_rows), earlier)
    before = before.reshape(NYC, all_rows).astype(jnp.int32)
    block = jnp.arange(all_rows, dtype=jnp.int32) // tok_rows
    slot = jnp.where(member > 0, before + block[None] * capacity, -1)
    chosen = slot[:, None, :] == lax.broadcasted_iota(jnp.int32, (NYC, span, all_rows), 1)
    zero = jnp.zeros((), BF16)
    pick = chosen.astype(BF16).reshape(NYC * span, all_rows)
    pick_high = jnp.where(chosen, weight_high[:, None, :], zero).reshape(NYC * span, all_rows)
    pick_low = jnp.where(chosen, weight_low[:, None, :], zero).reshape(NYC * span, all_rows)

    grad_rows = (dot(pick_high, cot_all) + dot(pick_low, cot_all)).astype(BF16)
    grad_rows, both = lax.optimization_barrier((grad_rows, both))
    grad_in = to_owner(grad_rows.reshape(NYC, span, features))
    send_rows = dot(pick, tok_all).astype(BF16)
    arrived = to_owner(send_rows.reshape(NYC, span, features))

    gate_w, up_w, down = w_gate[0], w_up[0], w_down[0]

    feature = jnp.arange(features, dtype=jnp.int32)
    f_row, f_c = feature % rows_sh, feature // rows_sh % NC
    f_zl, f_y = feature // (rows_sh * NC) % NZL, feature // (rows_sh * NC * NZL)
    came = ((f_y * NC + f_c) * NZL + f_zl) * rows_sh + f_row
    order = (
        came[:, None] == lax.broadcasted_iota(jnp.int32, (features, features), 1)
    ).astype(BF16)
    sh_join = dot(order, both).astype(BF16)

    sh_own, grad_in = reduce_over_dp(
        jnp.concatenate([dot(tok_all, sh_join), dot(cot_all, sh_down, 1, 1)], axis=1),
        direct=True,
        due=grad_in,
    )
    sh_own = sh_own[0]
    sh_gate_pre = sh_own[:, :part_sh]
    sh_up_pre = sh_own[:, part_sh : 2 * part_sh]
    sh_hidden = activate(sh_gate_pre, sh_up_pre)
    sh_pregrad = activation_grad(sh_gate_pre, sh_up_pre, sh_own[:, 2 * part_sh :])
    sh_full, addends = gather_over_dp(
        jnp.concatenate([sh_hidden, *sh_pregrad], axis=1).astype(BF16)[None],
        (1,),
        direct=True,
        due=(arrived, grad_in),
        then=lambda due: (
            dot(due[0].reshape(-1, features), gate_w),
            dot(due[0].reshape(-1, features), up_w),
            dot(due[1].reshape(-1, features), down, 1, 1),
        ),
    )
    sh_full = sh_full[0].reshape(all_rows, 3 * part_sh)
    slots = NYC * span
    arrived = arrived.reshape(slots, features)
    grad_in = grad_in.reshape(slots, features)
    sh_hidden_full = sh_full[:, :part_sh]
    sh_pregrad_full = sh_full[:, part_sh:]
    sh_grad = dot(tok_all, sh_pregrad_full, 0, 0).astype(BF16)
    sh_grad = dot(order, sh_grad, 0, 0).astype(BF16)
    sh_grad = to_owner(sh_grad.reshape(NYC, NZL * rows_sh, 2 * part_sh))
    sh_down_grad = dot(sh_hidden_full, cot_all, 0, 0).astype(BF16)
    sh_down_grad = to_owner(sh_down_grad.reshape(NYC, part_sh // NYC, features))
    own, (sh_grad, sh_down_grad) = reduce_over_dp(*addends, due=(sh_grad, sh_down_grad))
    gate_pre, up_pre, hidden_grad = own
    hidden_own = activate(gate_pre, up_pre)
    pregrad_own = activation_grad(gate_pre, up_pre, hidden_grad)
    sh_grad = jnp.sum(sh_grad.astype(F32), axis=0).astype(BF16)
    sh_grad = lax.all_to_all(
        sh_grad.reshape(NZL, rows_sh, 2 * part_sh), "zl", 0, 0, tiled=True
    )
    full, sh_grad = gather_over_dp(
        jnp.stack([hidden_own, *pregrad_own]).astype(BF16), (1, 1, 1), due=sh_grad
    )
    hidden_full, gate_full, up_full = [f.reshape(slots, hidden_exp) for f in full]

    expert_out = dot(hidden_full, down).astype(BF16)
    expert_out, hidden_late, grad_late = lax.optimization_barrier((expert_out, hidden_full, grad_in))
    grad_down = dot(hidden_late, grad_late, 0, 0).astype(BF16)[None]
    returned = to_owner(expert_out.reshape(NYC, span, features)).reshape(slots, features)
    out_part = (
        dot(sh_hidden_full, sh_down)
        + dot(pick_high, returned, 0, 0)
        + dot(pick_low, returned, 0, 0)
    )
    out_blocks = list(out_part.reshape(NZL, tok_rows, features))
    out_sent = send_near(out_blocks)

    input_grad = (dot(gate_full, gate_w, 1, 1) + dot(up_full, up_w, 1, 1)).astype(BF16)
    input_grad, grad_down = lax.optimization_barrier((input_grad, grad_down))
    grad_back = to_owner(input_grad.reshape(NYC, span, features)).reshape(slots, features)
    out_part, gate_late, arrived_late = lax.optimization_barrier((out_part, gate_full, arrived))
    grad_gate = dot(arrived_late, gate_late, 0, 0).astype(BF16)[None]
    out_sent[0], grad_gate, grad_back = lax.optimization_barrier((out_sent[0], grad_gate, grad_back))
    output = add_near(out_blocks, out_sent)
    tok_part = dot(sh_pregrad_full, sh_join, 1, 1) + dot(pick, grad_back, 0, 0)
    tok_blocks = list(tok_part.reshape(NZL, tok_rows, features))
    tok_sent = send_near(tok_blocks)
    tok_sent[0], up_late, arrived_late = lax.optimization_barrier(
        (tok_sent[0], up_full, arrived)
    )
    d_tokens = add_near(tok_blocks, tok_sent)

    grad_up = dot(arrived_late, up_late, 0, 0).astype(BF16)[None]

    def from_zl(g):
        g = g.reshape(NZL, rows_sh, NY, piece).transpose(1, 2, 0, 3)
        return g.reshape(rows_sh, hidden_sh)

    grad_shared_gate = from_zl(sh_grad[:, :, :part_sh])
    grad_shared_up = from_zl(sh_grad[:, :, part_sh:])
    grad_shared_down = jnp.sum(sh_down_grad.astype(F32), axis=0).astype(BF16)
    return (
        output,
        d_tokens,
        grad_gate,
        grad_up,
        grad_down,
        grad_shared_gate,
        grad_shared_up,
        grad_shared_down,
    )


def solution(mesh):
    parts = Mesh(
        mesh.devices.reshape(NX, NZH, NY, NZL, NC), ("x", "zh", "y", "zl", "c")
    )
    dp, expert = ("x", "zh"), ("y", "zl", "c")
    in_specs = (
        P(expert, dp),
        P(expert, None),
        P(expert, None),
        P(expert, dp, None),
        P(expert, dp, None),
        P(expert, None, dp),
        P(dp + expert, None),
        P(dp + expert, None),
        P(expert, dp),
        P(expert, dp),
    )
    out_specs = (
        P(expert, dp),
        P(expert, dp),
        P(expert, dp, None),
        P(expert, dp, None),
        P(expert, None, dp),
        P(dp + expert, None),
        P(dp + expert, None),
        P(expert, dp),
    )
    return jax.shard_map(
        body, mesh=parts, in_specs=in_specs, out_specs=out_specs, check_vma=False
    )
```
